32 devices in a mesh: dp: 2 (over y), row: 4 (over x, core), col: 4 (over z).
Axes of the slice: x: 2, y: 2, z: 4, core: 2. Of those that a mesh axis runs over, the one named last changes fastest.
Arguments:
- tokens: bfloat16 [1024, 1024], P(('dp', 'row'), 'col'), may hold values from -12 to 12
- cotangent: bfloat16 [1024, 1024], P(('dp', 'row'), 'col'), may hold values from -6 to 6
- first_gain: float32 [1024], P('col'), may hold values from 0.25 to 1.75
- first_shift: float32 [1024], P('col'), may hold values from -3 to 3
- w_qkv: bfloat16 [1024, 3072], P('col', 'row'), may hold values from -0.1875 to 0.1875
- bias_qv: float32 [2048], P('row'), may hold values from -4 to 4
- w_out: bfloat16 [1024, 1024], P('row', 'col'), may hold values from -0.375 to 0.375
- bias_out: float32 [1024], P('col'), may hold values from -3 to 3
- second_gain: float32 [1024], P('col'), may hold values from 0.25 to 1.75
- second_shift: float32 [1024], P('col'), may hold values from -3 to 3
- w_up: bfloat16 [1024, 4096], P('col', 'row'), may hold values from -0.1875 to 0.1875
- bias_up: float32 [4096], P('row'), may hold values from -4 to 4
- w_down: bfloat16 [4096, 1024], P('row', 'col'), may hold values from -0.125 to 0.125
- bias_down: float32 [1024], P('col'), may hold values from -3 to 3
Outputs:
- block_out: bfloat16 [1024, 1024], P(('dp', 'row'), 'col')
- grad_tokens: float32 [1024, 1024], P(('dp', 'row'), 'col')
- grad_first_gain: float32 [1024], P('col')
- grad_first_shift: float32 [1024], P('col')
- grad_w_qkv: float32 [1024, 3072], P('col', 'row')
- grad_bias_qv: float32 [2048], P('row')
- grad_w_out: float32 [1024, 1024], P('row', 'col')
- grad_bias_out: float32 [1024], P('col')
- grad_second_gain: float32 [1024], P('col')
- grad_second_shift: float32 [1024], P('col')
- grad_w_up: float32 [1024, 4096], P('col', 'row')
- grad_bias_up: float32 [4096], P('row')
- grad_w_down: float32 [4096, 1024], P('row', 'col')
- grad_bias_down: float32 [1024], P('col')
The draws below stay inside these ranges and needn't reach their ends.
All inputs are finite; a program needn't handle non-finite values.
Results may differ from the reference program's by a relative error of at most 0.012.
Values may be sent and summed in bfloat16 or wider, within the bound.
No kernel may reach another device: no remote copies, remote signals or barrier semaphores. Data moves between devices by JAX's collectives and lax.ppermute only.
A program may use at most 64 MiB of HBM per device.

```python
import jax
import jax.numpy as jnp
from jax import lax

D = 1024
HEADS = 16
HEAD_DIM = 64
FF = 4096
SEQ = 512
TOKENS = 1024


def draw_tokens(key, part):
    first_key = jax.random.fold_in(jax.random.fold_in(key, 7), 0)
    column_scale = 0.5 + jnp.arange(D).astype(jnp.float32) / (D - 1)
    drawn = jnp.clip(jax.random.normal(first_key, (TOKENS, D), jnp.float32), -4.0, 4.0)
    return (drawn * column_scale).astype(jnp.bfloat16)


def shard_levels(key, dims, pieces, low, largest):
    level, own = 1.0, jax.random.fold_in(key, 6)
    for dim, shards_of in pieces:
        steps = jnp.exp(jax.random.uniform(jax.random.fold_in(own, dim), (shards_of,), jnp.float32, low / len(pieces), largest / len(pieces)))
        level = level * jnp.repeat(steps, dims[dim] // shards_of).reshape([-1 if axis == dim else 1 for axis in range(len(dims))])
    return level


def gaussian(own_key, dims, scale, bound, cuts=(), kind=jnp.bfloat16):
    result = jax.random.normal(own_key, dims, jnp.float32) * scale
    if len(cuts) > 0:
        result = shard_levels(own_key, dims, cuts, -0.22, 0.18) * result
    return jnp.clip(result, min=-bound, max=bound).astype(kind)


def setup_inputs(seed: int = 0) -> dict:
    splits = jax.random.split(jax.random.key(seed), 15)
    return {
        "tokens": draw_tokens(jax.random.fold_in(splits[14], 71), 0),
        "cotangent": gaussian(splits[1], (TOKENS, D), 1.0, 6.0, ((0, 8), (1, 4))),
        "first_gain": jnp.clip(1.0 + 0.15 * jax.random.normal(splits[2], (D,), jnp.float32), 0.25, 1.75),
        "first_shift": gaussian(splits[3], (D,), 0.3, 3.0, ((0, 4),), jnp.float32),
        "w_qkv": gaussian(splits[4], (D, 3 * D), D ** -0.5, 0.1875, ((0, 4), (1, 4))),
        "bias_qv": gaussian(splits[5], (2 * D,), 0.5, 4.0, ((0, 4),), jnp.float32),
        "w_out": gaussian(splits[6], (D, D), (D // 4) ** -0.5, 0.375, ((0, 4), (1, 4))),
        "bias_out": gaussian(splits[7], (D,), 0.3, 3.0, ((0, 4),), jnp.float32),
        "second_gain": jnp.clip(1.0 + 0.15 * jax.random.normal(splits[8], (D,), jnp.float32), 0.25, 1.75),
        "second_shift": gaussian(splits[9], (D,), 0.3, 3.0, ((0, 4),), jnp.float32),
        "w_up": gaussian(splits[10], (D, FF), D ** -0.5, 0.1875, ((0, 4), (1, 4))),
        "bias_up": gaussian(splits[11], (FF,), 0.5, 4.0, ((0, 4),), jnp.float32),
        "w_down": gaussian(splits[12], (FF, D), (FF // 2) ** -0.5, 0.125, ((0, 4), (1, 4))),
        "bias_down": gaussian(splits[13], (D,), 0.3, 3.0, ((0, 4),), jnp.float32),
    }


EPS = 1e-05
GELU_C = 0.7978845608028654
GELU_A = 0.044715

def gelu_pair(hidden):
    inner = GELU_C * (hidden + GELU_A * hidden * hidden * hidden)
    tanh_val = jnp.tanh(inner)
    value = 0.5 * hidden * (1.0 + tanh_val)
    slope = 0.5 * (1.0 + tanh_val) + 0.5 * hidden * (1.0 - tanh_val * tanh_val) * GELU_C * (1.0 + 3.0 * GELU_A * hidden * hidden)
    return (value, slope)

def normalize(matrix, gain, shift):
    centre = lax.optimization_barrier(jnp.mean(matrix, -1, keepdims=True))
    spread = lax.optimization_barrier(jnp.mean(matrix * matrix, -1, keepdims=True)) - centre * centre
    rstd = lax.rsqrt(spread + EPS)
    normed = (matrix - centre) * rstd
    return (normed, rstd, (normed * gain + shift).astype(jnp.bfloat16))

def normalize_back(grad, normed, rstd, gain):
    scaled = grad * gain
    return rstd * (scaled - lax.optimization_barrier(jnp.mean(scaled, -1, keepdims=True)) - normed * lax.optimization_barrier(jnp.mean(scaled * normed, -1, keepdims=True)))

def fdot(left, right):
    return jnp.dot(left, right, preferred_element_type=jnp.float32)

def reference(tokens, cotangent, first_gain, first_shift, w_qkv, bias_qv, w_out, bias_out, second_gain, second_shift, w_up, bias_up, w_down, bias_down):
    seq_count = TOKENS // SEQ
    slopes = jnp.exp2(-8.0 * (jnp.arange(HEADS).astype(jnp.float32) + 1.0) / HEADS)
    positions = jnp.arange(SEQ).astype(jnp.int32)
    offsets = positions[:, None] - positions[None, :]
    causal_mask = offsets >= 0
    alibi = -slopes[:, None, None] * offsets.astype(jnp.float32)[None]
    bias_pair = bias_qv.reshape(HEADS, 2, HEAD_DIM)

    def one_seq(running, inputs):
        seq_tok, seq_cot = inputs
        inputs_f = seq_tok.astype(jnp.float32)
        normed_one, rstd_one, first_in = normalize(inputs_f, first_gain, first_shift)
        joined = fdot(first_in, w_qkv).reshape(SEQ, HEADS, 3, HEAD_DIM)
        queries = (joined[:, :, 0] + bias_pair[:, 0]).astype(jnp.bfloat16)
        keys_here = joined[:, :, 1].astype(jnp.bfloat16)
        values_here = (joined[:, :, 2] + bias_pair[:, 1]).astype(jnp.bfloat16)
        scores = jnp.einsum('qhe,khe->hqk', queries.astype(jnp.float32), keys_here.astype(jnp.float32)) * 0.125 + alibi
        scores = jnp.where(causal_mask[None], scores, -30000.0)
        exponent = jnp.exp(scores)
        row_total = lax.optimization_barrier(jnp.sum(exponent, -1))
        numerator = jnp.einsum('hqk,khe->qhe', exponent.astype(jnp.bfloat16).astype(jnp.float32), values_here.astype(jnp.float32))
        context = (numerator / row_total.T[:, :, None]).astype(jnp.bfloat16)
        logsum = jnp.log(row_total)
        context_flat = context.reshape(SEQ, D)
        resid = inputs_f + fdot(context_flat, w_out) + bias_out
        normed_two, rstd_two, second_in = normalize(resid, second_gain, second_shift)
        pre_act = fdot(second_in, w_up) + bias_up
        act, slope_act = gelu_pair(pre_act)
        act_b = act.astype(jnp.bfloat16)
        block_out = (resid + fdot(act_b, w_down) + bias_down).astype(jnp.bfloat16)
        cot_f = seq_cot.astype(jnp.float32)
        g_down = fdot(act_b.T, seq_cot)
        grad_pre = fdot(seq_cot, w_down.T) * slope_act
        grad_pre_b = grad_pre.astype(jnp.bfloat16)
        g_up = fdot(second_in.T, grad_pre_b)
        grad_second = fdot(grad_pre_b, w_up.T)
        grad_resid = cot_f + normalize_back(grad_second, normed_two, rstd_two, second_gain)
        resid_b = grad_resid.astype(jnp.bfloat16)
        g_out = fdot(context_flat.T, resid_b)
        grad_context = fdot(resid_b, w_out.T).astype(jnp.bfloat16).reshape(SEQ, HEADS, HEAD_DIM)
        grad_ctx_f = grad_context.astype(jnp.float32)
        delta = lax.optimization_barrier(jnp.sum(grad_ctx_f * context.astype(jnp.float32), -1)).T
        probs = jnp.exp(scores - logsum[:, :, None])
        dprob = jnp.einsum('qhe,khe->hqk', grad_ctx_f, values_here.astype(jnp.float32))
        dscore = (probs * (dprob - delta[:, :, None])).astype(jnp.bfloat16).astype(jnp.float32)
        grad_q = jnp.einsum('hqk,khe->qhe', dscore, keys_here.astype(jnp.float32)) * 0.125
        grad_k = jnp.einsum('hqk,qhe->khe', dscore, queries.astype(jnp.float32)) * 0.125
        grad_v = jnp.einsum('hqk,qhe->khe', probs.astype(jnp.bfloat16).astype(jnp.float32), grad_ctx_f)
        grad_joined = jnp.stack([grad_q, grad_k, grad_v], 2)
        g_bias_qv = lax.optimization_barrier(jnp.sum(jnp.stack([grad_q, grad_v], 2), 0)).reshape(-1)
        joined_b = grad_joined.reshape(SEQ, 3 * D).astype(jnp.bfloat16)
        g_qkv = fdot(first_in.T, joined_b)
        grad_first = fdot(joined_b, w_qkv.T)
        grad_tokens = grad_resid + normalize_back(grad_first, normed_one, rstd_one, first_gain)
        terms = (lax.optimization_barrier(jnp.sum(grad_first * normed_one, 0)), lax.optimization_barrier(jnp.sum(grad_first, 0)), g_qkv, g_bias_qv, g_out, lax.optimization_barrier(jnp.sum(grad_resid, 0)), lax.optimization_barrier(jnp.sum(grad_second * normed_two, 0)), lax.optimization_barrier(jnp.sum(grad_second, 0)), g_up, lax.optimization_barrier(jnp.sum(grad_pre, 0)), g_down, lax.optimization_barrier(jnp.sum(cot_f, 0)))
        running = tuple((old + new for old, new in zip(running, terms)))
        return (running, (block_out, grad_tokens))
    init = (jnp.zeros((D,), jnp.float32), jnp.zeros((D,), jnp.float32), jnp.zeros((D, 3 * D), jnp.float32), jnp.zeros((2 * D,), jnp.float32), jnp.zeros((D, D), jnp.float32), jnp.zeros((D,), jnp.float32), jnp.zeros((D,), jnp.float32), jnp.zeros((D,), jnp.float32), jnp.zeros((D, FF), jnp.float32), jnp.zeros((FF,), jnp.float32), jnp.zeros((FF, D), jnp.float32), jnp.zeros((D,), jnp.float32))
    totals, stacked = lax.scan(one_seq, init, (tokens.reshape(seq_count, SEQ, D), cotangent.reshape(seq_count, SEQ, D)))
    block_out = stacked[0].reshape(TOKENS, D)
    grad_tokens = stacked[1].reshape(TOKENS, D)
    return (block_out, grad_tokens, totals[0], totals[1], totals[2], totals[3], totals[4], totals[5], totals[6], totals[7], totals[8], totals[9], totals[10], totals[11])
```

```python
import jax
import jax.numpy as jnp
from jax import lax
from jax.sharding import PartitionSpec as P

HEADS = 16
HEAD_DIM = 64
SEQ = 512

EPS = 1e-05
GELU_C = 0.7978845608028654
GELU_A = 0.044715
BF16 = jnp.bfloat16
F32 = jnp.float32


def gelu_pair(hidden):
    inner = GELU_C * (hidden + GELU_A * hidden * hidden * hidden)
    tanh_val = jnp.tanh(inner)
    value = 0.5 * hidden * (1.0 + tanh_val)
    slope = 0.5 * (1.0 + tanh_val) + 0.5 * hidden * (1.0 - tanh_val * tanh_val) * GELU_C * (
        1.0 + 3.0 * GELU_A * hidden * hidden
    )
    return (value, slope)


def normalize(matrix, gain, shift):
    width = matrix.shape[1]
    centre = jnp.sum(matrix, 1, keepdims=True) / width
    spread = jnp.sum(matrix * matrix, 1, keepdims=True) / width - centre * centre
    rstd = lax.rsqrt(spread + EPS)
    normed = (matrix - centre) * rstd
    return (normed, rstd, (normed * gain + shift).astype(BF16))


def normalize_back(grad, normed, rstd, gain):
    width = grad.shape[1]
    scaled = grad * gain
    mean_one = jnp.sum(scaled, 1, keepdims=True) / width
    mean_two = jnp.sum(scaled * normed, 1, keepdims=True) / width
    return rstd * (scaled - mean_one - normed * mean_two)


def mm(left, right, left_dim, right_dim):
    return lax.dot_general(
        left, right, (((left_dim,), (right_dim,)), ((), ())), preferred_element_type=F32
    )


def shift(block, axis, step):
    size = lax.axis_size(axis)
    return lax.ppermute(block, axis, [(i, (i + step) % size) for i in range(size)])


def swap(block, axis, bit):
    size = lax.axis_size(axis)
    return lax.ppermute(block, axis, [(i, i ^ bit) for i in range(size)])


def split_pair(vector):
    high = vector.astype(BF16)
    return (high, (vector - high.astype(F32)).astype(BF16))


def exchange_col(pieces_of):
    size = lax.axis_size("col")
    own = lax.axis_index("col")
    return [pieces_of(own)] + [
        shift(pieces_of((own + step) % size), "col", step) for step in range(1, size)
    ]


def natural(pieces, axis):
    size = len(pieces)
    own = lax.axis_index("col")
    extent = pieces[0].shape[axis]
    order = pieces[::-1] + pieces[:0:-1]
    start = [jnp.int32(0)] * pieces[0].ndim
    start[axis] = (size - 1 - own) * extent
    sizes = list(pieces[0].shape)
    sizes[axis] = size * extent
    return lax.dynamic_slice(jnp.concatenate(order, axis), start, sizes)


def gather_col(block, axis):
    return natural(exchange_col(lambda index: block), axis)


def gather_row(block):
    bit = lax.axis_size("row") // 2
    while bit:
        block = jnp.concatenate([block, swap(block, "row", bit)], 0)
        bit //= 2
    return block


def scatter_row(partial):
    bit = 1
    while bit < lax.axis_size("row"):
        half = partial.shape[0] // 2
        partial = partial[:half] + swap(partial[half:].astype(BF16), "row", bit).astype(F32)
        bit *= 2
    return partial


def scatter_col(partial):
    own_rows = partial.shape[0] // lax.axis_size("col")

    def rows_of(index):
        return lax.dynamic_slice_in_dim(partial, index * own_rows, own_rows, 0)

    own = lax.axis_index("col")
    total = rows_of(own)
    for step in range(1, lax.axis_size("col")):
        piece = rows_of((own + step) % lax.axis_size("col")).astype(BF16)
        total = total + shift(piece, "col", step).astype(F32)
    return total


def sum_row(small):
    bit = 1
    while bit < lax.axis_size("row"):
        small = small + swap(small, "row", bit)
        bit *= 2
    return small


def sum_dp(small):
    bit = 1
    while bit < lax.axis_size("dp"):
        small = small + swap(small, "dp", bit)
        bit *= 2
    return small


def sum_dp_rounded(whole):
    bit = 1
    while bit < lax.axis_size("dp"):
        sent = whole.astype(BF16)
        whole = sent.astype(F32) + swap(sent, "dp", bit).astype(F32)
        bit *= 2
    return whole


def after(value, *others):
    return lax.optimization_barrier((value, *others))[0]


def local(
    tokens,
    cotangent,
    first_gain,
    first_shift,
    w_qkv,
    bias_qv,
    w_out,
    bias_out,
    second_gain,
    second_shift,
    w_up,
    bias_up,
    w_down,
    bias_down,
):
    cols = lax.axis_size("col")
    rows = lax.axis_size("row")
    own_col = lax.axis_index("col")
    own_row = lax.axis_index("row")
    rows_a, feats = tokens.shape
    rows_t = rows_a // cols
    head_count = bias_qv.shape[0] // (2 * HEAD_DIM)
    own_heads = head_count // cols
    qkv_cols = w_qkv.shape[1] // cols
    ff_cols = w_up.shape[1] // cols
    out_rows = w_out.shape[0] // cols

    vectors = [first_gain, first_shift, bias_out, second_gain, second_shift, bias_down]
    vector_rows = [part for vector in vectors for part in split_pair(vector)]
    vector_rows += [jnp.zeros((feats,), BF16)] * (-len(vector_rows) % 16)
    head_block = jnp.concatenate([tokens, jnp.stack(vector_rows)], 0)
    gathered = gather_col(head_block, 1)
    x_rows = gathered[:rows_a].astype(F32)
    whole_vectors = [
        gathered[rows_a + 2 * i].astype(F32) + gathered[rows_a + 2 * i + 1].astype(F32)
        for i in range(len(vectors))
    ]
    gain_one, shift_one, out_bias, gain_two, shift_two, down_bias = whole_vectors

    wq = natural(
        exchange_col(
            lambda index: lax.dynamic_slice_in_dim(w_qkv, index * qkv_cols, qkv_cols, 1)
        ),
        0,
    )

    normed_one, rstd_one, first_in = normalize(x_rows, gain_one, shift_one)
    first_all = gather_row(first_in)

    w_up_g, w_down_g, w_out_g, cot_g = lax.optimization_barrier(
        (w_up, w_down, w_out, cotangent, gathered)
    )[:4]

    def weight_piece(index):
        return jnp.concatenate(
            [
                lax.dynamic_slice_in_dim(w_up_g, index * ff_cols, ff_cols, 1),
                lax.dynamic_slice_in_dim(w_down_g, index * ff_cols, ff_cols, 0).T,
                lax.dynamic_slice_in_dim(w_out_g, index * out_rows, out_rows, 0).T,
            ],
            1,
        )

    weights = natural(exchange_col(weight_piece), 0)
    w_up_s = weights[:, :ff_cols]
    w_down_t = weights[:, ff_cols : 2 * ff_cols]
    w_out_t = weights[:, 2 * ff_cols :]
    cot_rows = gather_col(cot_g, 1)
    cot_all = gather_row(cot_rows)

    joined = mm(first_all, wq, 1, 0).reshape(-1, own_heads, 3, HEAD_DIM)
    bias_own = lax.dynamic_slice_in_dim(
        bias_qv.reshape(head_count, 2, HEAD_DIM), own_col * own_heads, own_heads, 0
    )
    queries = (joined[:, :, 0] + bias_own[:, 0]).astype(BF16)
    keys = joined[:, :, 1].astype(BF16)
    values = (joined[:, :, 2] + bias_own[:, 1]).astype(BF16)
    block_ids = jnp.zeros((1,), jnp.int32) + own_row
    bit = rows // 2
    while bit:
        block_ids = jnp.concatenate([block_ids, block_ids ^ bit])
        bit //= 2
    pos = (block_ids[:, None] * rows_a + jnp.arange(rows_a, dtype=jnp.int32)[None]).reshape(-1)
    head_ids = own_row * head_count + own_col * own_heads + jnp.arange(own_heads, dtype=jnp.int32)
    slopes = jnp.exp2(-8.0 * (head_ids.astype(F32) + 1.0) / HEADS)
    offsets = pos[:, None] - pos[None, :]
    mask = (offsets >= 0) & (pos[:, None] // SEQ == pos[None, :] // SEQ)
    scores = jnp.einsum("qhe,khe->hqk", queries, keys, preferred_element_type=F32) * 0.125
    scores = scores - slopes[:, None, None] * offsets.astype(F32)[None]
    scores = jnp.where(mask[None], scores, -30000.0)
    expo = jnp.exp(scores)
    row_total = jnp.sum(expo, -1)
    numerator = jnp.einsum("hqk,khe->qhe", expo.astype(BF16), values, preferred_element_type=F32)
    context = (numerator / row_total.T[:, :, None]).astype(BF16)
    context_flat = context.reshape(-1, own_heads * HEAD_DIM)

    def own_tokens(whole):
        return lax.dynamic_slice_in_dim(whole, own_col * rows_t, rows_t, 0)

    mixed = scatter_col(scatter_row(mm(context_flat, w_out_t, 1, 1)))
    resid = own_tokens(x_rows) + mixed + out_bias
    normed_two, rstd_two, second_in = normalize(resid, gain_two, shift_two)
    second_all = gather_row(gather_col(second_in, 0))

    bias_up_own = lax.dynamic_slice_in_dim(bias_up, own_col * ff_cols, ff_cols, 0)
    pre_act = mm(second_all, w_up_s, 1, 0) + bias_up_own
    act_f, slope_act = gelu_pair(pre_act)
    act = act_f.astype(BF16)
    grad_pre = mm(cot_all, w_down_t, 1, 0) * slope_act
    up_bias_part = jnp.sum(grad_pre, 0)
    grad_pre_b = grad_pre.astype(BF16)
    grad_second = scatter_col(scatter_row(mm(grad_pre_b, w_up_s, 1, 1)))
    out_part = scatter_col(scatter_row(mm(act, w_down_t, 1, 1)))
    block_rows = (resid + out_part + down_bias).astype(BF16)

    def features_of(whole, index):
        return lax.dynamic_slice_in_dim(whole, index * feats, feats, 1)

    block_out = natural(exchange_col(lambda index: features_of(block_rows, index)), 0)

    cot_own = own_tokens(cot_rows).astype(F32)
    grad_resid = cot_own + normalize_back(grad_second, normed_two, rstd_two, gain_two)
    resid_all = gather_row(gather_col(grad_resid.astype(BF16), 0))
    grad_context = mm(resid_all, w_out_t, 1, 0).astype(BF16).reshape(-1, own_heads, HEAD_DIM)

    probs = jnp.exp(scores - jnp.log(row_total)[:, :, None])
    delta = jnp.sum(grad_context.astype(F32) * context.astype(F32), -1).T
    dprob = jnp.einsum("qhe,khe->hqk", grad_context, values, preferred_element_type=F32)
    dscore = (probs * (dprob - delta[:, :, None])).astype(BF16)
    grad_q = jnp.einsum("hqk,khe->qhe", dscore, keys, preferred_element_type=F32) * 0.125
    grad_k = jnp.einsum("hqk,qhe->khe", dscore, queries, preferred_element_type=F32) * 0.125
    grad_v = jnp.einsum(
        "hqk,qhe->khe", probs.astype(BF16), grad_context, preferred_element_type=F32
    )
    joined_f = jnp.stack([grad_q, grad_k, grad_v], 2)
    qv_bias_part = jnp.sum(jnp.stack([grad_q, grad_v], 2), 0).reshape(-1)
    joined_b = joined_f.reshape(joined_f.shape[0], -1).astype(BF16)
    grad_first = scatter_col(scatter_row(mm(joined_b, wq, 1, 1)))
    grad_tokens_t = grad_resid + normalize_back(
        grad_first, own_tokens(normed_one), own_tokens(rstd_one), gain_one
    )

    sums = jnp.stack(
        [
            jnp.sum(grad_first * own_tokens(normed_one), 0),
            jnp.sum(grad_first, 0),
            jnp.sum(grad_second * normed_two, 0),
            jnp.sum(grad_second, 0),
            jnp.sum(grad_resid, 0),
            jnp.sum(cot_own, 0),
        ]
    )
    sums = jnp.concatenate([sums, jnp.zeros((-sums.shape[0] % 8, sums.shape[1]), F32)], 0)
    last = jnp.concatenate([grad_tokens_t, sums], 0)
    last_pieces = exchange_col(lambda index: features_of(last, index))
    grad_tokens = natural([piece[:rows_t] for piece in last_pieces], 0)
    col_sums = natural([piece[rows_t:] for piece in last_pieces], 0)
    col_sums = jnp.sum(col_sums.reshape(cols, -1, feats), 0)
    col_sums = sum_dp(sum_row(col_sums))

    narrow = sum_dp(jnp.concatenate([up_bias_part, qv_bias_part])[None])
    narrow = gather_col(narrow, 0)
    grad_bias_up = narrow[:, : up_bias_part.shape[0]].reshape(-1)
    grad_bias_qv = narrow[:, up_bias_part.shape[0] :].reshape(-1)

    grad_down_t = mm(cot_all, act, 0, 0)
    grad_up = mm(second_all, grad_pre_b, 0, 0)
    ff_grads = sum_dp_rounded(jnp.concatenate([grad_up, grad_down_t], 1)).astype(BF16)

    def feature_rows(whole, index):
        return lax.dynamic_slice_in_dim(whole, index * feats, feats, 0)

    ff_pieces = exchange_col(lambda index: feature_rows(ff_grads, index))
    grad_w_up = natural([piece[:, :ff_cols] for piece in ff_pieces], 1).astype(F32)
    grad_w_down = natural([piece[:, ff_cols:].T for piece in ff_pieces], 0).astype(F32)
    grad_out_t = sum_dp_rounded(mm(resid_all, context_flat, 0, 0)).astype(BF16)
    out_pieces = exchange_col(lambda index: feature_rows(grad_out_t, index))
    grad_w_out = natural([piece.T for piece in out_pieces], 0).astype(F32)
    grad_qkv = sum_dp_rounded(mm(first_all, joined_b, 0, 0)).astype(BF16)
    grad_w_qkv = natural(exchange_col(lambda index: feature_rows(grad_qkv, index)), 1).astype(F32)

    return (
        block_out,
        grad_tokens,
        col_sums[0],
        col_sums[1],
        grad_w_qkv,
        grad_bias_qv,
        grad_w_out,
        col_sums[4],
        col_sums[2],
        col_sums[3],
        grad_w_up,
        grad_bias_up,
        grad_w_down,
        col_sums[5],
    )


def solution(mesh):
    tokens_spec = P(("dp", "row"), "col")
    placed = (
        tokens_spec,
        tokens_spec,
        P("col"),
        P("col"),
        P("col", "row"),
        P("row"),
        P("row", "col"),
        P("col"),
        P("col"),
        P("col"),
        P("col", "row"),
        P("row"),
        P("row", "col"),
        P("col"),
    )
    return jax.shard_map(
        local,
        mesh=mesh,
        in_specs=placed,
        out_specs=(
            tokens_spec,
            tokens_spec,
            P("col"),
            P("col"),
            P("col", "row"),
            P("row"),
            P("row", "col"),
            P("col"),
            P("col"),
            P("col"),
            P("col", "row"),
            P("row"),
            P("row", "col"),
            P("col"),
        ),
        check_vma=False,
    )
```

```python
import functools

import jax
import jax.numpy as jnp
from jax import lax
from jax.experimental import pallas as pl
from jax.experimental.pallas import tpu as pltpu
from jax.sharding import PartitionSpec as P

HEADS = 16
HEAD_DIM = 64
SEQ = 512

EPS = 1e-05
GELU_C = 0.7978845608028654
GELU_A = 0.044715
BF16 = jnp.bfloat16
F32 = jnp.float32
PAD = 16


VM = pl.BlockSpec(memory_space=pltpu.VMEM)
SM = pl.BlockSpec(memory_space=pltpu.SMEM)


def call(body, outs, place, *args, flops=0, scratch=(), name=None):
    shapes = [jax.ShapeDtypeStruct(shape, kind) for shape, kind in outs]
    moved = sum(a.size * a.dtype.itemsize for a in args)
    moved += sum(s.size * s.dtype.itemsize for s in shapes)
    return pl.pallas_call(
        body,
        out_shape=shapes,
        in_specs=[SM] + [VM] * len(args),
        out_specs=[VM] * len(shapes),
        scratch_shapes=list(scratch),
        name=name,
        cost_estimate=pl.CostEstimate(flops=flops, bytes_accessed=moved, transcendentals=0),
    )(place, *args)


def mm(left, right, left_dim, right_dim):
    return lax.dot_general(
        left, right, (((left_dim,), (right_dim,)), ((), ())), preferred_element_type=F32
    )


def part(index, extent):
    return pl.ds(pl.multiple_of(index * extent, extent), extent)


def source(place, step, cols):
    return lax.rem(place[0] + cols - step, cols)


def target(place, step, cols):
    return lax.rem(place[0] + step, cols)


def split_rows(values):
    high = values.astype(BF16)
    return (high, (values - high.astype(F32)).astype(BF16))


def block_order(rows):
    order = [0]
    bit = rows // 2
    while bit:
        order = order + [o ^ bit for o in order]
        bit //= 2
    return order


def positions(place, order, extent, axis):
    shape = (extent, 1) if axis == 0 else (1, extent)
    pieces = [
        lax.broadcasted_iota(jnp.int32, shape, axis) + jnp.bitwise_xor(place[1], o) * extent
        for o in order
    ]
    return pieces if axis == 0 else jnp.concatenate(pieces, axis)


def shift(block, axis, step):
    size = lax.axis_size(axis)
    return lax.ppermute(block, axis, [(i, (i + step) % size) for i in range(size)])


def swap(block, axis, bit):
    size = lax.axis_size(axis)
    return lax.ppermute(block, axis, [(i, i ^ bit) for i in range(size)])


def exchange(blocks):
    return [blocks[0]] + [shift(blocks[s], "col", s) for s in range(1, len(blocks))]


def gather_row(block):
    pieces = [block]
    bit = lax.axis_size("row") // 2
    while bit:
        pieces = pieces + [swap(piece, "row", bit) for piece in pieces]
        bit //= 2
    return pieces


def sum_small(small, axis):
    bit = 1
    while bit < lax.axis_size(axis):
        small = small + swap(small, axis, bit)
        bit *= 2
    return small


def swap_dp(message):
    size = lax.axis_size("dp")
    bit = 1
    while bit < size // 2:
        message = (message.astype(F32) + swap(message, "dp", bit).astype(F32)).astype(BF16)
        bit *= 2
    return (message, swap(message, "dp", bit))


def head_kernel(place, tokens, *refs):
    vectors, out = refs[:-1], refs[-1]
    rows = tokens.shape[0]
    out[:rows] = tokens[...]
    stacked = jnp.concatenate(
        [v[...] for v in vectors] + [jnp.zeros((8 - len(vectors), tokens.shape[1]), F32)], 0
    )
    high, low = split_rows(stacked)
    out[rows:] = jnp.concatenate([high.astype(F32), low.astype(F32)], 0).astype(BF16)


def qkv_pieces_kernel(place, w_qkv, w_out, *outs):
    cols = len(outs)
    width = w_qkv.shape[1] // cols
    height = w_out.shape[0] // cols
    for step, out in enumerate(outs):
        for k in range(cols):

            @pl.when(target(place, step, cols) == k)
            def _(out=out, k=k):
                out[:, :width] = w_qkv[:, k * width : (k + 1) * width]
                out[:, width:] = w_out[k * height : (k + 1) * height].astype(F32).T.astype(BF16)


def ff_pieces_kernel(place, cotangent, w_up, w_down, *outs):
    cols = len(outs)
    width = w_up.shape[1] // cols
    high = w_up.shape[0]
    for step, out in enumerate(outs):
        index = target(place, step, cols)
        out[:high] = w_up[:, part(index, width)]
        out[high : high + width] = w_down[part(index, width), :]
        out[high + width :] = cotangent[...]


def first_norm_kernel(place, *refs):
    cols = (len(refs) - 5) // 1
    pieces, (first_in, normed_out, rstd_out, x_out, vec_out) = refs[:cols], refs[cols:]
    rows = first_in.shape[0]
    feats = pieces[0].shape[1]
    for step, piece in enumerate(pieces):
        at = part(source(place, step, cols), feats)
        x_out[:, at] = piece[:rows]
        tail = piece[rows:].astype(F32)
        vec_out[:, at] = tail[:8] + tail[8:]
    x = x_out[...].astype(F32)
    width = x.shape[1]
    centre = jnp.sum(x, 1, keepdims=True) / width
    spread = jnp.sum(x * x, 1, keepdims=True) / width - centre * centre
    rstd = lax.rsqrt(spread + EPS)
    normed = (x - centre) * rstd
    normed_out[...] = normed
    rstd_out[...] = rstd
    first_in[...] = (normed * vec_out[0:1] + vec_out[1:2]).astype(BF16)


def attention_kernel(order, heads, cols, place, slopes, bias, *refs):
    rows = len(order)
    first, weights = refs[:rows], refs[rows : rows + cols]
    q_out, k_out, v_out, log_out, ctx_out, wq_out, wo_out, keep, send = refs[rows + cols :]
    feats = weights[0].shape[0]
    width = wq_out.shape[1]
    for step, piece in enumerate(weights):
        at = part(source(place, step, cols), feats)
        wq_out[at, :] = piece[:, :width]
        wo_out[at, :] = piece[:, width:]
    extent = first[0].shape[0]
    own_bias = bias[:, part(place[0], 2 * heads * HEAD_DIM)]
    for p in range(rows):
        joined = mm(first[p][...], wq_out[...], 1, 0)
        at = slice(p * extent, (p + 1) * extent)
        for h in range(heads):
            here = slice(h * HEAD_DIM, (h + 1) * HEAD_DIM)
            base = 3 * h * HEAD_DIM
            b = 2 * h * HEAD_DIM
            q = joined[:, base : base + HEAD_DIM] + own_bias[:, b : b + HEAD_DIM]
            v = joined[:, base + 2 * HEAD_DIM : base + 3 * HEAD_DIM]
            v = v + own_bias[:, b + HEAD_DIM : b + 2 * HEAD_DIM]
            q_out[at, here] = q.astype(BF16)
            k_out[at, here] = joined[:, base + HEAD_DIM : base + 2 * HEAD_DIM].astype(BF16)
            v_out[at, here] = v.astype(BF16)
    for p in range(rows):
        at = slice(p * extent, (p + 1) * extent)
        for h in range(heads):
            here = slice(h * HEAD_DIM, (h + 1) * HEAD_DIM)
            scores = block_scores(place, order, extent, p, q_out[at, here], k_out[:, here], slopes[h])
            expo = jnp.exp(scores)
            total = jnp.sum(expo, 1, keepdims=True)
            log_out[at, h : h + 1] = jnp.log(total)
            numerator = mm(expo.astype(BF16), v_out[:, here], 1, 0)
            ctx_out[at, here] = (numerator / total).astype(BF16)
    half = keep.shape[0]
    keep[...] = mm(ctx_out[:half], wo_out[...], 1, 1)
    send[...] = mm(ctx_out[half:], wo_out[...], 1, 1).astype(BF16)


def block_scores(place, order, extent, p, query, keys, slope):
    query_pos = positions(place, order[p : p + 1], extent, 0)[0]
    key_pos = positions(place, order, extent, 1)
    offsets = query_pos - key_pos
    same = lax.div(query_pos, jnp.int32(SEQ)) == lax.div(key_pos, jnp.int32(SEQ))
    scores = mm(query, keys, 1, 1) * 0.125 - slope * offsets.astype(F32)
    return jnp.where((offsets >= 0) & same, scores, -30000.0)


def probs_kernel(order, heads, place, slopes, q, k, logs, out):
    rows = len(order)
    extent = q.shape[0] // rows
    for h in range(heads):
        here = slice(h * HEAD_DIM, (h + 1) * HEAD_DIM)
        for p in range(rows):
            at = slice(p * extent, (p + 1) * extent)
            scores = block_scores(place, order, extent, p, q[at, here], k[:, here], slopes[h])
            out[h, at, :] = jnp.exp(scores - logs[at, h : h + 1])


def fold_kernel(place, keep, recv, keep_out, send_out):
    half = keep_out.shape[0]
    keep_out[...] = keep[:half] + recv[:half].astype(F32)
    send_out[...] = (keep[half:] + recv[half:].astype(F32)).astype(BF16)


def to_tokens_kernel(place, keep, recv, own, *sends):
    cols = len(sends) + 1
    count = own.shape[0]
    for step, out in enumerate((own, *sends)):
        at = part(target(place, step, cols), count)
        out[...] = (keep[at, :] + recv[at, :].astype(F32)).astype(out.dtype)


def total_of(own, received):
    total = own[...]
    for piece in received:
        total = total + piece[...].astype(F32)
    return total


def second_norm_kernel(place, own, *refs):
    received, (x, vec, resid_out, normed_out, rstd_out, second_in) = refs[:-6], refs[-6:]
    count = own.shape[0]
    x_own = x[part(place[0], count), :].astype(F32)
    resid = x_own + total_of(own, received) + vec[2:3]
    width = resid.shape[1]
    centre = jnp.sum(resid, 1, keepdims=True) / width
    spread = jnp.sum(resid * resid, 1, keepdims=True) / width - centre * centre
    rstd = lax.rsqrt(spread + EPS)
    normed = (resid - centre) * rstd
    resid_out[...] = resid
    normed_out[...] = normed
    rstd_out[...] = rstd
    second_in[...] = (normed * vec[3:4] + vec[4:5]).astype(BF16)


def join_rows_kernel(place, *refs):
    pieces, out = refs[:-1], refs[-1]
    count = pieces[0].shape[0]
    for step, piece in enumerate(pieces):
        out[part(source(place, step, len(pieces)), count), :] = piece[...]


def ff_join_kernel(place, *refs):
    pieces, (up_out, down_out, cot_out) = refs[:-3], refs[-3:]
    cols = len(pieces)
    feats = pieces[0].shape[1] if cot_out.shape[1] == cols * pieces[0].shape[1] else 0
    high = up_out.shape[0] // cols
    width = down_out.shape[0]
    for step, piece in enumerate(pieces):
        at = part(source(place, step, cols), feats)
        up_out[at, :] = piece[:high]
        down_out[:, at] = piece[high : high + width]
        cot_out[:, at] = piece[high + width :]


def cot_kernel(place, down, *refs):
    pieces, out = refs[:-1], refs[-1]
    extent = pieces[0].shape[0]
    for p, piece in enumerate(pieces):
        out[p * extent : (p + 1) * extent] = mm(piece[...], down[...], 1, 1)


def hidden_kernel(place, up, bias, cot_down, *refs):
    pieces, (act_out, grad_out, bias_out, keep, send) = refs[:-5], refs[-5:]
    extent = pieces[0].shape[0]
    width = up.shape[1]
    own_bias = bias[:, part(place[0], width)]
    bias_total = jnp.zeros((1, width), F32)
    for p, piece in enumerate(pieces):
        at = slice(p * extent, (p + 1) * extent)
        hidden = mm(piece[...], up[...], 1, 0) + own_bias
        inner = GELU_C * (hidden + GELU_A * hidden * hidden * hidden)
        tanh_val = jnp.tanh(inner)
        act_out[at] = (0.5 * hidden * (1.0 + tanh_val)).astype(BF16)
        slope = 0.5 * (1.0 + tanh_val) + 0.5 * hidden * (1.0 - tanh_val * tanh_val) * GELU_C * (
            1.0 + 3.0 * GELU_A * hidden * hidden
        )
        grad_pre = cot_down[at] * slope
        bias_total = bias_total + jnp.sum(grad_pre, 0, keepdims=True)
        grad_out[at] = grad_pre.astype(BF16)
    bias_out[...] = bias_total
    half = keep.shape[0]
    keep[...] = mm(grad_out[:half], up[...], 1, 1)
    send[...] = mm(grad_out[half:], up[...], 1, 1).astype(BF16)


def out_part_kernel(place, act, down, keep, send):
    half = keep.shape[0]
    keep[...] = mm(act[:half], down[...], 1, 0)
    send[...] = mm(act[half:], down[...], 1, 0).astype(BF16)


def out_features_kernel(place, keep, recv, resid, own, *refs):
    sends, total = refs[:-1], refs[-1]
    cols = len(sends) + 1
    feats = own.shape[1]
    total[...] = keep[...] + recv[...].astype(F32)
    mine = part(place[0], resid.shape[0])
    total[mine, :] = total[mine, :] + resid[...]
    for step, out in enumerate((own, *sends)):
        out[...] = total[:, part(target(place, step, cols), feats)].astype(out.dtype)


def block_out_kernel(place, bias, own, *refs):
    received, out = refs[:-1], refs[-1]
    out[...] = (total_of(own, received) + bias[...]).astype(BF16)


def ff_grad_kernel(rows, cols, place, act, grad, bias, *refs):
    second, cots, out = refs[:rows], refs[rows : 2 * rows], refs[-1]
    extent = second[0].shape[0]
    feats = second[0].shape[1] // cols
    width = grad.shape[1]
    stride = feats + width
    for j in range(cols):
        here = slice(j * feats, (j + 1) * feats)
        up = jnp.zeros((feats, width), F32)
        down = jnp.zeros((width, feats), F32)
        for p in range(rows):
            at = slice(p * extent, (p + 1) * extent)
            up = up + mm(second[p][:, here], grad[at], 0, 0)
            down = down + mm(act[at], cots[p][:, here], 0, 0)
        out[j * stride : j * stride + feats] = up.astype(BF16)
        out[j * stride + feats : (j + 1) * stride] = down.astype(BF16)
    out[cols * stride :] = pair_rows(bias[...])


def pair_rows(vector):
    high, low = split_rows(vector)
    empty = jnp.zeros((PAD - 2, vector.shape[1]), F32)
    return jnp.concatenate([high.astype(F32), low.astype(F32), empty], 0).astype(BF16)


def dp_sum_kernel(place, mine, other, own, *sends):
    cols = len(sends) + 1
    stride = own.shape[0] - PAD
    tail = cols * stride
    ends = mine[tail:].astype(F32) + other[tail:].astype(F32)
    both = ends[0:1] + ends[1:2]
    for step, out in enumerate((own, *sends)):
        at = part(target(place, step, cols), stride)
        out[:stride] = (mine[at, :].astype(F32) + other[at, :].astype(F32)).astype(out.dtype)
        out[stride:] = pair_rows(both).astype(out.dtype)


def ff_final_kernel(place, *refs):
    pieces, (up_out, down_out, bias_out) = refs[:-3], refs[-3:]
    cols = len(pieces)
    feats = down_out.shape[1]
    width = up_out.shape[1] // cols
    for step, piece in enumerate(pieces):
        at = part(source(place, step, cols), width)
        up_out[:, at] = piece[:feats].astype(F32)
        down_out[at, :] = piece[feats : feats + width].astype(F32)
        tail = piece[feats + width :].astype(F32)
        bias_out[:, at] = tail[0:1] + tail[1:2]


def second_back_kernel(place, own, *refs):
    received = refs[:-7]
    normed, rstd, vec, cot, resid_out, resid_b, sums = refs[-7:]
    count = own.shape[0]
    grad = total_of(own, received)
    n = normed[...]
    width = grad.shape[1]
    scaled = grad * vec[3:4]
    mean_one = jnp.sum(scaled, 1, keepdims=True) / width
    mean_two = jnp.sum(scaled * n, 1, keepdims=True) / width
    cot_own = cot[part(place[0], count), :].astype(F32)
    resid = cot_own + rstd[...] * (scaled - mean_one - n * mean_two)
    resid_out[...] = resid
    resid_b[...] = resid.astype(BF16)
    sums[0:1] = jnp.sum(grad * n, 0, keepdims=True)
    sums[1:2] = jnp.sum(grad, 0, keepdims=True)
    sums[2:3] = jnp.sum(resid, 0, keepdims=True)
    sums[3:4] = jnp.sum(cot_own, 0, keepdims=True)
    sums[4:8] = jnp.zeros((4, width), F32)


def attention_back_kernel(rows, heads, place, wq, wo, q, k, v, ctx, probs, *refs):
    resid = refs[:rows]
    joined_out, bias_out, keep, send, gctx = refs[rows:]
    extent = resid[0].shape[0]
    for p in range(rows):
        at = slice(p * extent, (p + 1) * extent)
        gctx[at] = mm(resid[p][...], wo[...], 1, 0).astype(BF16)
    for h in range(heads):
        here = slice(h * HEAD_DIM, (h + 1) * HEAD_DIM)
        base = 3 * h * HEAD_DIM
        size = q.shape[0]
        grad_k = jnp.zeros((size, HEAD_DIM), F32)
        grad_v = jnp.zeros((size, HEAD_DIM), F32)
        bias_q = jnp.zeros((1, HEAD_DIM), F32)
        for p in range(rows):
            at = slice(p * extent, (p + 1) * extent)
            grad = gctx[at, here]
            delta = jnp.sum(grad.astype(F32) * ctx[at, here].astype(F32), 1, keepdims=True)
            prob = probs[h, at, :]
            dscore = (prob * (mm(grad, v[:, here], 1, 1) - delta)).astype(BF16)
            grad_q = mm(dscore, k[:, here], 1, 0) * 0.125
            bias_q = bias_q + jnp.sum(grad_q, 0, keepdims=True)
            joined_out[at, base : base + HEAD_DIM] = grad_q.astype(BF16)
            grad_k = grad_k + mm(dscore, q[at, here], 0, 0)
            grad_v = grad_v + mm(prob.astype(BF16), grad, 0, 0)
        joined_out[:, base + HEAD_DIM : base + 2 * HEAD_DIM] = (grad_k * 0.125).astype(BF16)
        joined_out[:, base + 2 * HEAD_DIM : base + 3 * HEAD_DIM] = grad_v.astype(BF16)
        b = 2 * h * HEAD_DIM
        bias_out[:, b : b + HEAD_DIM] = bias_q
        bias_out[:, b + HEAD_DIM : b + 2 * HEAD_DIM] = jnp.sum(grad_v, 0, keepdims=True)
    half = keep.shape[0]
    keep[...] = mm(joined_out[:half], wq[...], 1, 1)
    send[...] = mm(joined_out[half:], wq[...], 1, 1).astype(BF16)


def qkv_grad_kernel(rows, place, joined, ctx, bias, *refs):
    first, resid, out = refs[:rows], refs[rows : 2 * rows], refs[-1]
    extent = first[0].shape[0]
    width = joined.shape[1]
    high = first[0].shape[1]
    grad = jnp.zeros((high, width), F32)
    grad_out = jnp.zeros((high, ctx.shape[1]), F32)
    for p in range(rows):
        at = slice(p * extent, (p + 1) * extent)
        grad = grad + mm(first[p][...], joined[at], 0, 0)
        grad_out = grad_out + mm(resid[p][...], ctx[at], 0, 0)
    out[:high, :width] = grad.astype(BF16)
    out[:high, width:] = grad_out.astype(BF16)
    rest = out.shape[1] - bias.shape[1]
    row = jnp.concatenate([bias[...], jnp.zeros((1, rest), F32)], 1)
    out[high:] = pair_rows(row)


def qkv_final_kernel(place, *refs):
    pieces, (qkv_out, out_out, bias_out) = refs[:-3], refs[-3:]
    cols = len(pieces)
    feats = qkv_out.shape[0]
    width = qkv_out.shape[1] // cols
    high = out_out.shape[0] // cols
    bias = bias_out.shape[1] // cols
    for step, piece in enumerate(pieces):
        index = source(place, step, cols)
        for k in range(cols):

            @pl.when(index == k)
            def _(piece=piece, k=k):
                qkv_out[:, k * width : (k + 1) * width] = piece[:feats, :width].astype(F32)

        out_out[part(index, high), :] = piece[:feats, width:].astype(F32).T
        tail = piece[feats:, :bias].astype(F32)
        bias_out[:, part(index, bias)] = tail[0:1] + tail[1:2]


def first_back_kernel(place, keep, recv, normed, rstd, vec, resid, sums, own, *refs):
    sends, total = refs[:-1], refs[-1]
    cols = len(sends) + 1
    feats = own.shape[1]
    extent, width = keep.shape
    grad = keep[...] + recv[...].astype(F32)
    n = normed[...]
    scaled = grad * vec[0:1]
    one = jnp.sum(scaled, 1, keepdims=True) / width
    two = jnp.sum(scaled * n, 1, keepdims=True) / width
    total[:extent] = rstd[...] * scaled
    mine = part(place[0], resid.shape[0])
    total[mine, :] = total[mine, :] + resid[...]
    gain_sum = jnp.sum(grad * n, 0, keepdims=True)
    shift_sum = jnp.sum(grad, 0, keepdims=True)
    lane = lax.broadcasted_iota(jnp.int32, (extent, 128), 1)
    stats = jnp.where(lane == 0, one, jnp.where(lane == 1, two, 0.0)).T[:2]
    stats = jnp.concatenate([stats, jnp.zeros((2, feats - extent), F32)], 1)
    tail = total.at[extent : extent + 8]
    tail[0:4] = sums[0:4]
    tail[4:5] = gain_sum
    tail[5:6] = shift_sum
    for step, out in enumerate((own, *sends)):
        at = part(target(place, step, cols), feats)
        out[:extent] = total[:extent, at].astype(out.dtype)
        ends = jnp.concatenate([tail[0:6, at], stats], 0)
        high, low = split_rows(ends)
        out[extent:] = jnp.concatenate([high.astype(F32), low.astype(F32)], 0).astype(out.dtype)


def tokens_final_kernel(place, normed, rstd, own, *refs):
    received, (out, sums) = refs[:-2], refs[-2:]
    extent, feats = out.shape
    total = total_of(own, received)
    ends = total[extent : extent + 8] + total[extent + 8 : extent + 16]
    sums[...] = ends
    lanes = jnp.concatenate([ends[6:8, :extent], jnp.zeros((6, extent), F32)], 0)
    square = jnp.concatenate([lanes, jnp.zeros((120, extent), F32)], 0).T
    n = normed[:, part(place[0], feats)]
    out[...] = total[:extent] - rstd[...] * (square[:, 0:1] + n * square[:, 1:2])


def scatter_row(keep, send, place, name):
    bit = 1
    while bit < lax.axis_size("row") // 2:
        recv = swap(send, "row", bit)
        half = (keep.shape[0] // 2, keep.shape[1])
        keep, send = call(fold_kernel, [(half, F32), (half, BF16)], place, keep, recv, name=name)
        bit *= 2
    return (keep, swap(send, "row", bit))


def local(
    tokens,
    cotangent,
    first_gain,
    first_shift,
    w_qkv,
    bias_qv,
    w_out,
    bias_out,
    second_gain,
    second_shift,
    w_up,
    bias_up,
    w_down,
    bias_down,
):
    cols = lax.axis_size("col")
    rows = lax.axis_size("row")
    own_col = lax.axis_index("col")
    own_row = lax.axis_index("row")
    place = jnp.stack([own_col, own_row]).astype(jnp.int32)
    extent, feats = tokens.shape
    width = feats * cols
    group = extent * rows
    half = group // 2
    count = extent // cols
    head_count = bias_qv.shape[0] // (2 * HEAD_DIM)
    heads = head_count // cols
    qkv_cols = w_qkv.shape[1] // cols
    ff_cols = w_up.shape[1] // cols
    out_rows = w_out.shape[0] // cols
    order = block_order(rows)
    head_ids = own_row * head_count + own_col * heads + jnp.arange(heads, dtype=jnp.int32)
    slopes = jnp.exp2(-8.0 * (head_ids.astype(F32) + 1.0) / HEADS)

    vectors = [first_gain, first_shift, bias_out, second_gain, second_shift]
    (head_block,) = call(
        head_kernel,
        [((extent + PAD, feats), BF16)],
        place,
        tokens,
        *[v.reshape(1, -1) for v in vectors],
        name="head",
    )
    heads_in = exchange([head_block] * cols)
    qkv_blocks = call(
        qkv_pieces_kernel,
        [((feats, qkv_cols + out_rows), BF16)] * cols,
        place,
        w_qkv,
        w_out,
        name="qkv_pieces",
    )
    qkv_in = exchange(qkv_blocks)
    first_in, normed_one, rstd_one, x_rows, vec = call(
        first_norm_kernel,
        [
            ((extent, width), BF16),
            ((extent, width), F32),
            ((extent, 1), F32),
            ((extent, width), BF16),
            ((8, width), F32),
        ],
        place,
        *heads_in,
        name="first_norm",
    )
    first_all = gather_row(first_in)

    cot_late, up_late, down_late = lax.optimization_barrier(
        (cotangent, w_up, w_down, first_in)
    )[:3]
    ff_blocks = call(
        ff_pieces_kernel,
        [((feats + ff_cols + extent, feats), BF16)] * cols,
        place,
        cot_late,
        up_late,
        down_late,
        name="ff_pieces",
    )
    ff_in = exchange(ff_blocks)

    wide = (group, heads * HEAD_DIM)
    partial_outs = [((half, width), F32), ((half, width), BF16)]
    body = functools.partial(attention_kernel, order, heads, cols)

    def attention_body(place_ref, slopes_ref, *refs):
        body(place_ref, slopes_ref, *refs)

    q, k, v, logs, context, wq, wo, keep, send = call_slopes(
        attention_body,
        [
            (wide, BF16),
            (wide, BF16),
            (wide, BF16),
            ((group, heads), F32),
            (wide, BF16),
            ((width, qkv_cols), BF16),
            ((width, out_rows), BF16),
        ]
        + partial_outs,
        place,
        slopes,
        bias_qv.reshape(1, -1),
        *first_all,
        *qkv_in,
        name="attention",
    )
    keep, recv = scatter_row(keep, send, place, "fold_context")
    own, *sends = call(
        to_tokens_kernel,
        [((count, width), F32)] + [((count, width), BF16)] * (cols - 1),
        place,
        keep,
        recv,
        name="context_tokens",
    )
    received = exchange([own, *sends])[1:]
    resid, normed_two, rstd_two, second_in = call(
        second_norm_kernel,
        [
            ((count, width), F32),
            ((count, width), F32),
            ((count, 1), F32),
            ((count, width), BF16),
        ],
        place,
        own,
        *received,
        x_rows,
        vec,
        name="second_norm",
    )
    (second_rows,) = call(
        join_rows_kernel,
        [((extent, width), BF16)],
        place,
        *exchange([second_in] * cols),
        name="join_second",
    )
    second_all = gather_row(second_rows)

    w_up_s, w_down_s, cot_rows = call(
        ff_join_kernel,
        [((width, ff_cols), BF16), ((ff_cols, width), BF16), ((extent, width), BF16)],
        place,
        *ff_in,
        name="ff_join",
    )
    cot_all = gather_row(cot_rows)
    (cot_down,) = call(
        cot_kernel,
        [((group, ff_cols), F32)],
        place,
        w_down_s,
        *cot_all,
        name="cot_down",
        flops=2 * group * width * ff_cols,
    )
    (probs,) = call_slopes(
        functools.partial(probs_kernel, order, heads),
        [((heads, group, group), F32)],
        place,
        slopes,
        q,
        k,
        logs,
        name="probs",
    )

    act, grad_pre, up_bias_part, keep, send = call(
        hidden_kernel,
        [((group, ff_cols), BF16), ((group, ff_cols), BF16), ((1, ff_cols), F32)] + partial_outs,
        place,
        w_up_s,
        bias_up.reshape(1, -1),
        cot_down,
        *second_all,
        name="hidden",
        flops=4 * group * width * ff_cols,
    )
    keep, recv = scatter_row(keep, send, place, "fold_second")
    own, *sends = call(
        to_tokens_kernel,
        [((count, width), F32)] + [((count, width), BF16)] * (cols - 1),
        place,
        keep,
        recv,
        name="second_tokens",
    )
    received = exchange([own, *sends])[1:]
    grad_resid, resid_b, sums = call(
        second_back_kernel,
        [((count, width), F32), ((count, width), BF16), ((8, width), F32)],
        place,
        own,
        *received,
        normed_two,
        rstd_two,
        vec,
        cot_rows,
        name="second_back",
    )
    (resid_rows,) = call(
        join_rows_kernel,
        [((extent, width), BF16)],
        place,
        *exchange([resid_b] * cols),
        name="join_resid",
    )
    resid_all = gather_row(resid_rows)

    keep, send = call(
        out_part_kernel,
        partial_outs,
        place,
        act,
        w_down_s,
        name="out_part",
        flops=2 * group * width * ff_cols,
    )
    keep, recv = scatter_row(keep, send, place, "fold_out")
    own, *sends = call(
        out_features_kernel,
        [((extent, feats), F32)] + [((extent, feats), BF16)] * (cols - 1),
        place,
        keep,
        recv,
        resid,
        scratch=[pltpu.VMEM((extent, width), F32)],
        name="out_features",
    )
    (block_out,) = call(
        block_out_kernel,
        [((extent, feats), BF16)],
        place,
        bias_down.reshape(1, -1),
        own,
        *exchange([own, *sends])[1:],
        name="block_out",
    )

    (ff_message,) = call(
        functools.partial(ff_grad_kernel, rows, cols),
        [((cols * (feats + ff_cols) + PAD, ff_cols), BF16)],
        place,
        act,
        grad_pre,
        up_bias_part,
        *second_all,
        *cot_all,
        name="ff_grad",
        flops=4 * group * width * ff_cols,
    )
    ff_shape = (feats + ff_cols + PAD, ff_cols)
    ff_sums = call(
        dp_sum_kernel,
        [(ff_shape, F32)] + [(ff_shape, BF16)] * (cols - 1),
        place,
        *swap_dp(ff_message),
        name="ff_dp",
    )
    grad_w_up, grad_w_down, grad_bias_up = call(
        ff_final_kernel,
        [(w_up.shape, F32), (w_down.shape, F32), ((1, bias_up.shape[0]), F32)],
        place,
        *exchange(ff_sums),
        name="ff_final",
    )

    joined, qv_bias_part, keep, send = call(
        functools.partial(attention_back_kernel, rows, heads),
        [((group, qkv_cols), BF16), ((1, 2 * heads * HEAD_DIM), F32)] + partial_outs,
        place,
        wq,
        wo,
        q,
        k,
        v,
        context,
        probs,
        *resid_all,
        scratch=[pltpu.VMEM(wide, BF16)],
        name="attention_back",
    )
    (qkv_message,) = call(
        functools.partial(qkv_grad_kernel, rows),
        [((width + PAD, qkv_cols + out_rows), BF16)],
        place,
        joined,
        context,
        qv_bias_part,
        *first_all,
        *resid_all,
        name="qkv_grad",
        flops=2 * group * width * (qkv_cols + out_rows),
    )
    qkv_shape = (feats + PAD, qkv_cols + out_rows)
    qkv_sums = call(
        dp_sum_kernel,
        [(qkv_shape, F32)] + [(qkv_shape, BF16)] * (cols - 1),
        place,
        *swap_dp(qkv_message),
        name="qkv_dp",
    )
    grad_w_qkv, grad_w_out, grad_bias_qv = call(
        qkv_final_kernel,
        [(w_qkv.shape, F32), (w_out.shape, F32), ((1, bias_qv.shape[0]), F32)],
        place,
        *exchange(qkv_sums),
        name="qkv_final",
    )

    keep, recv = scatter_row(keep, send, place, "fold_first")
    last_shape = (extent + PAD, feats)
    last = call(
        first_back_kernel,
        [(last_shape, F32)] + [(last_shape, BF16)] * (cols - 1),
        place,
        keep,
        recv,
        normed_one,
        rstd_one,
        vec,
        grad_resid,
        sums,
        scratch=[pltpu.VMEM((extent + 8, width), F32)],
        name="first_back",
    )
    grad_tokens, col_sums = call(
        tokens_final_kernel,
        [((extent, feats), F32), ((8, feats), F32)],
        place,
        normed_one,
        rstd_one,
        *exchange(last),
        name="tokens_final",
    )
    col_sums = sum_small(sum_small(col_sums, "row"), "dp")

    return (
        block_out,
        grad_tokens,
        col_sums[4],
        col_sums[5],
        grad_w_qkv,
        grad_bias_qv.reshape(-1),
        grad_w_out,
        col_sums[2],
        col_sums[0],
        col_sums[1],
        grad_w_up,
        grad_bias_up.reshape(-1),
        grad_w_down,
        col_sums[3],
    )


def call_slopes(body, outs, place, slopes, *args, name):
    shapes = [jax.ShapeDtypeStruct(shape, kind) for shape, kind in outs]
    moved = sum(a.size * a.dtype.itemsize for a in args)
    moved += sum(s.size * s.dtype.itemsize for s in shapes)
    return pl.pallas_call(
        body,
        out_shape=shapes,
        in_specs=[SM, SM] + [VM] * len(args),
        out_specs=[VM] * len(shapes),
        name=name,
        cost_estimate=pl.CostEstimate(flops=1 << 31, bytes_accessed=moved, transcendentals=1 << 19),
    )(place, slopes, *args)


def solution(mesh):
    tokens_spec = P(("dp", "row"), "col")
    vector = P("col")
    placed = (
        tokens_spec,
        tokens_spec,
        vector,
        vector,
        P("col", "row"),
        P("row"),
        P("row", "col"),
        vector,
        vector,
        vector,
        P("col", "row"),
        P("row"),
        P("row", "col"),
        vector,
    )
    return jax.shard_map(
        local,
        mesh=mesh,
        in_specs=placed,
        out_specs=(
            tokens_spec,
            tokens_spec,
            vector,
            vector,
            P("col", "row"),
            P("row"),
            P("row", "col"),
            vector,
            vector,
            vector,
            P("col", "row"),
            P("row"),
            P("row", "col"),
            vector,
        ),
        check_vma=False,
    )
```

```python
import functools

import jax
import jax.numpy as jnp
from jax import lax
from jax.experimental import pallas as pl
from jax.experimental.pallas import tpu as pltpu
from jax.sharding import PartitionSpec as P


HEADS = 16
HEAD_DIM = 64
SEQ = 512

EPS = 1e-05
GELU_C = 0.7978845608028654
GELU_A = 0.044715
BF16 = jnp.bfloat16
F32 = jnp.float32
PAD = 16
GRANT = 12 << 20


VM = pl.BlockSpec(memory_space=pltpu.VMEM)
SM = pl.BlockSpec(memory_space=pltpu.SMEM)
HB = pl.BlockSpec(memory_space=pltpu.HBM)


def call(body, outs, place, *args, flops=0, scratch=(), hbm=()):
    shapes = [jax.ShapeDtypeStruct(shape, kind) for shape, kind in outs]
    moved = sum(a.size * a.dtype.itemsize for a in args)
    moved += sum(s.size * s.dtype.itemsize for s in shapes)
    return pl.pallas_call(
        body,
        out_shape=shapes,
        in_specs=[SM] + [HB if i in hbm else VM for i in range(len(args))],
        out_specs=[VM] * len(shapes),
        scratch_shapes=list(scratch),
        compiler_params=pltpu.CompilerParams(vmem_limit_bytes=GRANT),
        cost_estimate=pl.CostEstimate(flops=flops, bytes_accessed=moved, transcendentals=0),
    )(place, *args)


def mm(left, right, left_dim, right_dim):
    return lax.dot_general(
        left, right, (((left_dim,), (right_dim,)), ((), ())), preferred_element_type=F32
    )


def part(index, extent):
    return pl.ds(pl.multiple_of(index * extent, extent), extent)


def source(place, step, cols):
    return lax.rem(place[0] + cols - step, cols)


def target(place, step, cols):
    return lax.rem(place[0] + step, cols)


def split_rows(values):
    high = values.astype(BF16)
    return (high, (values - high.astype(F32)).astype(BF16))


def block_order(rows):
    order = [0]
    bit = rows // 2
    while bit:
        order = order + [o ^ bit for o in order]
        bit //= 2
    return order


def positions(place, order, extent, axis):
    shape = (extent, 1) if axis == 0 else (1, extent)
    pieces = [
        lax.broadcasted_iota(jnp.int32, shape, axis) + jnp.bitwise_xor(place[1], o) * extent
        for o in order
    ]
    return pieces if axis == 0 else jnp.concatenate(pieces, axis)


def shift(block, axis, step):
    size = lax.axis_size(axis)
    return lax.ppermute(block, axis, [(i, (i + step) % size) for i in range(size)])


def swap(block, axis, bit):
    size = lax.axis_size(axis)
    return lax.ppermute(block, axis, [(i, i ^ bit) for i in range(size)])


def exchange(blocks):
    return [blocks[0]] + [shift(blocks[s], "col", s) for s in range(1, len(blocks))]


def gather_row(block):
    pieces = [block]
    bit = lax.axis_size("row") // 2
    while bit:
        for i in range(len(pieces)):
            pieces = pieces + [swap(pieces[i], "row", bit)]
        bit //= 2
    return pieces


def sum_small(small, axis):
    bit = 1
    while bit < lax.axis_size(axis):
        small = small + swap(small, axis, bit)
        bit *= 2
    return small


def swap_dp(message):
    size = lax.axis_size("dp")
    bit = 1
    while bit < size // 2:
        message = (message.astype(F32) + swap(message, "dp", bit).astype(F32)).astype(BF16)
        bit *= 2
    return (message, swap(message, "dp", bit))


def head_kernel(tokens, vectors, out):
    rows = tokens.shape[0]
    out[:rows] = tokens[...]
    high, low = split_rows(vectors[...])
    out[rows:] = jnp.concatenate([high.astype(F32), low.astype(F32)], 0).astype(BF16)


def qkv_pieces_kernel(place, w_qkv_hbm, w_out_hbm, *refs):
    outs, (w_qkv, w_out, sems) = refs[:-3], refs[-3:]
    copies = [
        pltpu.make_async_copy(w_qkv_hbm, w_qkv, sems.at[0]),
        pltpu.make_async_copy(w_out_hbm, w_out, sems.at[1]),
    ]
    for copy in copies:
        copy.start()
    for copy in copies:
        copy.wait()
    cols = len(outs)
    width = w_qkv.shape[1] // cols
    height = w_out.shape[0] // cols
    for step, out in enumerate(outs):
        for k in range(cols):

            @pl.when(target(place, step, cols) == k)
            def _(out=out, k=k):
                out[:, :width] = w_qkv[:, k * width : (k + 1) * width]
                out[:, width:] = w_out[k * height : (k + 1) * height].astype(F32).T.astype(BF16)


def ff_pieces_kernel(place, cotangent, w_up, w_down, *refs):
    outs, sems = refs[:-1], refs[-1]
    cols = len(outs)
    width = w_up.shape[1] // cols
    high = w_up.shape[0]
    copies = []
    for step, out in enumerate(outs):
        index = target(place, step, cols)
        pairs = [
            (w_up.at[:, part(index, width)], out.at[:high]),
            (w_down.at[part(index, width), :], out.at[high : high + width]),
            (cotangent, out.at[high + width :]),
        ]
        for i, (there, here) in enumerate(pairs):
            copies.append(pltpu.make_async_copy(there, here, sems.at[3 * step + i]))
    for copy in copies:
        copy.start()
    for copy in copies:
        copy.wait()


def first_norm_kernel(place, *refs):
    cols = (len(refs) - 5) // 1
    pieces, (first_in, normed_out, rstd_out, x_out, vec_out) = refs[:cols], refs[cols:]
    rows = first_in.shape[0]
    feats = pieces[0].shape[1]
    for step, piece in enumerate(pieces):
        at = part(source(place, step, cols), feats)
        x_out[:, at] = piece[:rows]
        tail = piece[rows:].astype(F32)
        vec_out[:, at] = tail[:8] + tail[8:]
    x = x_out[...].astype(F32)
    width = x.shape[1]
    centre = jnp.sum(x, 1, keepdims=True) / width
    spread = jnp.sum(x * x, 1, keepdims=True) / width - centre * centre
    rstd = lax.rsqrt(spread + EPS)
    normed = (x - centre) * rstd
    normed_out[...] = normed
    rstd_out[...] = rstd
    first_in[...] = (normed * vec_out[0:1] + vec_out[1:2]).astype(BF16)


def attention_kernel(order, heads, cols, place, slopes, bias, *refs):
    rows = len(order)
    first, weights = refs[:rows], refs[rows : rows + cols]
    q_out, k_out, v_out, log_out, ctx_out, wq_out, wo_out, keep, send = refs[rows + cols :]
    feats = weights[0].shape[0]
    width = wq_out.shape[1]
    for step, piece in enumerate(weights):
        at = part(source(place, step, cols), feats)
        wq_out[at, :] = piece[:, :width]
        wo_out[at, :] = piece[:, width:]
    extent = first[0].shape[0]
    own_bias = bias[:, part(place[0], 2 * heads * HEAD_DIM)]
    for p in range(rows):
        joined = mm(first[p][...], wq_out[...], 1, 0)
        at = slice(p * extent, (p + 1) * extent)
        for h in range(heads):
            here = slice(h * HEAD_DIM, (h + 1) * HEAD_DIM)
            base = 3 * h * HEAD_DIM
            b = 2 * h * HEAD_DIM
            q = joined[:, base : base + HEAD_DIM] + own_bias[:, b : b + HEAD_DIM]
            v = joined[:, base + 2 * HEAD_DIM : base + 3 * HEAD_DIM]
            v = v + own_bias[:, b + HEAD_DIM : b + 2 * HEAD_DIM]
            q_out[at, here] = q.astype(BF16)
            k_out[at, here] = joined[:, base + HEAD_DIM : base + 2 * HEAD_DIM].astype(BF16)
            v_out[at, here] = v.astype(BF16)
    for p in range(rows):
        at = slice(p * extent, (p + 1) * extent)
        for h in range(heads):
            here = slice(h * HEAD_DIM, (h + 1) * HEAD_DIM)
            scores = block_scores(place, order, extent, p, q_out[at, here], k_out[:, here], slopes[h])
            expo = jnp.exp(scores)
            total = jnp.sum(expo, 1, keepdims=True)
            log_out[at, h : h + 1] = jnp.log(total)
            numerator = mm(expo.astype(BF16), v_out[:, here], 1, 0)
            ctx_out[at, here] = (numerator / total).astype(BF16)
    half = keep.shape[0]
    keep[...] = mm(ctx_out[:half], wo_out[...], 1, 1)
    send[...] = mm(ctx_out[half:], wo_out[...], 1, 1).astype(BF16)


def block_scores(place, order, extent, p, query, keys, slope):
    query_pos = positions(place, order[p : p + 1], extent, 0)[0]
    key_pos = positions(place, order, extent, 1)
    offsets = query_pos - key_pos
    same = lax.div(query_pos, jnp.int32(SEQ)) == lax.div(key_pos, jnp.int32(SEQ))
    scores = mm(query, keys, 1, 1) * 0.125 - slope * offsets.astype(F32)
    return jnp.where((offsets >= 0) & same, scores, -30000.0)


def probs_kernel(order, heads, place, slopes, q, k, logs, out):
    rows = len(order)
    extent = q.shape[0] // rows
    for h in range(heads):
        here = slice(h * HEAD_DIM, (h + 1) * HEAD_DIM)
        for p in range(rows):
            at = slice(p * extent, (p + 1) * extent)
            scores = block_scores(place, order, extent, p, q[at, here], k[:, here], slopes[h])
            out[h, at, :] = jnp.exp(scores - logs[at, h : h + 1])


def fold_kernel(place, keep, recv, keep_out, send_out):
    half = keep_out.shape[0]
    keep_out[...] = keep[:half] + recv[:half].astype(F32)
    send_out[...] = (keep[half:] + recv[half:].astype(F32)).astype(BF16)


def to_tokens_kernel(place, keep, recv, own, *sends):
    cols = len(sends) + 1
    count = own.shape[0]
    for step, out in enumerate((own, *sends)):
        at = part(target(place, step, cols), count)
        out[...] = (keep[at, :] + recv[at, :].astype(F32)).astype(out.dtype)


def total_of(own, received):
    total = own[...]
    for piece in received:
        total = total + piece[...].astype(F32)
    return total


def second_norm_kernel(place, own, *refs):
    received, (x, vec, resid_out, normed_out, rstd_out, second_in) = refs[:-6], refs[-6:]
    count = own.shape[0]
    x_own = x[part(place[0], count), :].astype(F32)
    resid = x_own + total_of(own, received) + vec[2:3]
    width = resid.shape[1]
    centre = jnp.sum(resid, 1, keepdims=True) / width
    spread = jnp.sum(resid * resid, 1, keepdims=True) / width - centre * centre
    rstd = lax.rsqrt(spread + EPS)
    normed = (resid - centre) * rstd
    resid_out[...] = resid
    normed_out[...] = normed
    rstd_out[...] = rstd
    second_in[...] = (normed * vec[3:4] + vec[4:5]).astype(BF16)


def join_rows_kernel(place, *refs):
    pieces, out = refs[:-1], refs[-1]
    count = pieces[0].shape[0]
    for step, piece in enumerate(pieces):
        out[part(source(place, step, len(pieces)), count), :] = piece[...]


def ff_join_kernel(place, *refs):
    pieces, (up_out, down_out, cot_out) = refs[:-3], refs[-3:]
    cols = len(pieces)
    feats = pieces[0].shape[1] if cot_out.shape[1] == cols * pieces[0].shape[1] else 0
    high = up_out.shape[0] // cols
    width = down_out.shape[0]
    for step, piece in enumerate(pieces):
        at = part(source(place, step, cols), feats)
        up_out[at, :] = piece[:high]
        down_out[:, at] = piece[high : high + width]
        cot_out[:, at] = piece[high + width :]


def cot_kernel(place, down, *refs):
    pieces, out = refs[:-1], refs[-1]
    extent = pieces[0].shape[0]
    for p, piece in enumerate(pieces):
        out[p * extent : (p + 1) * extent] = mm(piece[...], down[...], 1, 1)


def hidden_kernel(place, up, bias, cot_down, *refs):
    pieces, (act_out, grad_out, bias_out, keep, send) = refs[:-5], refs[-5:]
    extent = pieces[0].shape[0]
    width = up.shape[1]
    own_bias = bias[:, part(place[0], width)]
    bias_total = jnp.zeros((1, width), F32)
    for p, piece in enumerate(pieces):
        at = slice(p * extent, (p + 1) * extent)
        hidden = mm(piece[...], up[...], 1, 0) + own_bias
        inner = GELU_C * (hidden + GELU_A * hidden * hidden * hidden)
        tanh_val = jnp.tanh(inner)
        act_out[at] = (0.5 * hidden * (1.0 + tanh_val)).astype(BF16)
        slope = 0.5 * (1.0 + tanh_val) + 0.5 * hidden * (1.0 - tanh_val * tanh_val) * GELU_C * (
            1.0 + 3.0 * GELU_A * hidden * hidden
        )
        grad_pre = cot_down[at] * slope
        bias_total = bias_total + jnp.sum(grad_pre, 0, keepdims=True)
        grad_out[at] = grad_pre.astype(BF16)
    bias_out[...] = bias_total
    half = keep.shape[0]
    keep[...] = mm(grad_out[:half], up[...], 1, 1)
    send[...] = mm(grad_out[half:], up[...], 1, 1).astype(BF16)


def out_part_kernel(place, act, down, keep, send):
    half = keep.shape[0]
    keep[...] = mm(act[:half], down[...], 1, 0)
    send[...] = mm(act[half:], down[...], 1, 0).astype(BF16)


def out_features_kernel(place, keep, recv, resid, own, *refs):
    sends, total = refs[:-1], refs[-1]
    cols = len(sends) + 1
    feats = own.shape[1]
    total[...] = keep[...] + recv[...].astype(F32)
    mine = part(place[0], resid.shape[0])
    total[mine, :] = total[mine, :] + resid[...]
    for step, out in enumerate((own, *sends)):
        out[...] = total[:, part(target(place, step, cols), feats)].astype(out.dtype)


def block_out_kernel(place, bias, own, *refs):
    received, out = refs[:-1], refs[-1]
    out[...] = (total_of(own, received) + bias[...]).astype(BF16)


def ff_grad_kernel(rows, cols, place, act, grad, bias, *refs):
    second, cots, out = refs[:rows], refs[rows : 2 * rows], refs[-1]
    extent = second[0].shape[0]
    feats = second[0].shape[1] // cols
    width = grad.shape[1]
    stride = feats + width
    for j in range(cols):
        here = slice(j * feats, (j + 1) * feats)
        up = jnp.zeros((feats, width), F32)
        down = jnp.zeros((width, feats), F32)
        for p in range(rows):
            at = slice(p * extent, (p + 1) * extent)
            up = up + mm(second[p][:, here], grad[at], 0, 0)
            down = down + mm(act[at], cots[p][:, here], 0, 0)
        out[j * stride : j * stride + feats] = up.astype(BF16)
        out[j * stride + feats : (j + 1) * stride] = down.astype(BF16)
    out[cols * stride :] = pair_rows(bias[...])


def pair_rows(vector):
    high, low = split_rows(vector)
    empty = jnp.zeros((PAD - 2, vector.shape[1]), F32)
    return jnp.concatenate([high.astype(F32), low.astype(F32), empty], 0).astype(BF16)


def dp_sum_kernel(place, mine, other, own, *sends):
    cols = len(sends) + 1
    stride = own.shape[0] - PAD
    tail = cols * stride
    ends = mine[tail:].astype(F32) + other[tail:].astype(F32)
    both = ends[0:1] + ends[1:2]
    for step, out in enumerate((own, *sends)):
        at = part(target(place, step, cols), stride)
        out[:stride] = (mine[at, :].astype(F32) + other[at, :].astype(F32)).astype(out.dtype)
        out[stride:] = pair_rows(both).astype(out.dtype)


def ff_final_kernel(place, *refs):
    pieces, (up_out, down_out, bias_out) = refs[:-3], refs[-3:]
    cols = len(pieces)
    feats = down_out.shape[1]
    width = up_out.shape[1] // cols
    for step, piece in enumerate(pieces):
        at = part(source(place, step, cols), width)
        up_out[:, at] = piece[:feats].astype(F32)
        down_out[at, :] = piece[feats : feats + width].astype(F32)
        tail = piece[feats + width :].astype(F32)
        bias_out[:, at] = tail[0:1] + tail[1:2]


def second_back_kernel(place, own, *refs):
    received = refs[:-7]
    normed, rstd, vec, cot, resid_out, resid_b, sums = refs[-7:]
    count = own.shape[0]
    grad = total_of(own, received)
    n = normed[...]
    width = grad.shape[1]
    scaled = grad * vec[3:4]
    mean_one = jnp.sum(scaled, 1, keepdims=True) / width
    mean_two = jnp.sum(scaled * n, 1, keepdims=True) / width
    cot_own = cot[part(place[0], count), :].astype(F32)
    resid = cot_own + rstd[...] * (scaled - mean_one - n * mean_two)
    resid_out[...] = resid
    resid_b[...] = resid.astype(BF16)
    sums[0:1] = jnp.sum(grad * n, 0, keepdims=True)
    sums[1:2] = jnp.sum(grad, 0, keepdims=True)
    sums[2:3] = jnp.sum(resid, 0, keepdims=True)
    sums[3:4] = jnp.sum(cot_own, 0, keepdims=True)
    sums[4:8] = jnp.zeros((4, width), F32)


def attention_back_kernel(rows, heads, place, wq, wo, q, k, v, ctx, probs, *refs):
    resid = refs[:rows]
    joined_out, bias_out, keep, send, gctx = refs[rows:]
    extent = resid[0].shape[0]
    for p in range(rows):
        at = slice(p * extent, (p + 1) * extent)
        gctx[at] = mm(resid[p][...], wo[...], 1, 0).astype(BF16)
    for h in range(heads):
        here = slice(h * HEAD_DIM, (h + 1) * HEAD_DIM)
        base = 3 * h * HEAD_DIM
        size = q.shape[0]
        grad_k = jnp.zeros((size, HEAD_DIM), F32)
        grad_v = jnp.zeros((size, HEAD_DIM), F32)
        bias_q = jnp.zeros((1, HEAD_DIM), F32)
        for p in range(rows):
            at = slice(p * extent, (p + 1) * extent)
            grad = gctx[at, here]
            delta = jnp.sum(grad.astype(F32) * ctx[at, here].astype(F32), 1, keepdims=True)
            prob = probs[h, at, :]
            dscore = (prob * (mm(grad, v[:, here], 1, 1) - delta)).astype(BF16)
            grad_q = mm(dscore, k[:, here], 1, 0) * 0.125
            bias_q = bias_q + jnp.sum(grad_q, 0, keepdims=True)
            joined_out[at, base : base + HEAD_DIM] = grad_q.astype(BF16)
            grad_k = grad_k + mm(dscore, q[at, here], 0, 0)
            grad_v = grad_v + mm(prob.astype(BF16), grad, 0, 0)
        joined_out[:, base + HEAD_DIM : base + 2 * HEAD_DIM] = (grad_k * 0.125).astype(BF16)
        joined_out[:, base + 2 * HEAD_DIM : base + 3 * HEAD_DIM] = grad_v.astype(BF16)
        b = 2 * h * HEAD_DIM
        bias_out[:, b : b + HEAD_DIM] = bias_q
        bias_out[:, b + HEAD_DIM : b + 2 * HEAD_DIM] = jnp.sum(grad_v, 0, keepdims=True)
    half = keep.shape[0]
    keep[...] = mm(joined_out[:half], wq[...], 1, 1)
    send[...] = mm(joined_out[half:], wq[...], 1, 1).astype(BF16)


def qkv_grad_kernel(rows, place, joined, ctx, bias, *refs):
    first, resid, out = refs[:rows], refs[rows : 2 * rows], refs[-1]
    extent = first[0].shape[0]
    width = joined.shape[1]
    high = first[0].shape[1]
    grad = jnp.zeros((high, width), F32)
    grad_out = jnp.zeros((high, ctx.shape[1]), F32)
    for p in range(rows):
        at = slice(p * extent, (p + 1) * extent)
        grad = grad + mm(first[p][...], joined[at], 0, 0)
        grad_out = grad_out + mm(resid[p][...], ctx[at], 0, 0)
    out[:high, :width] = grad.astype(BF16)
    out[:high, width:] = grad_out.astype(BF16)
    rest = out.shape[1] - bias.shape[1]
    row = jnp.concatenate([bias[...], jnp.zeros((1, rest), F32)], 1)
    out[high:] = pair_rows(row)


def qkv_final_kernel(place, *refs):
    pieces, (qkv_out, out_out, bias_out) = refs[:-3], refs[-3:]
    cols = len(pieces)
    feats = qkv_out.shape[0]
    width = qkv_out.shape[1] // cols
    high = out_out.shape[0] // cols
    bias = bias_out.shape[1] // cols
    for step, piece in enumerate(pieces):
        index = source(place, step, cols)
        for k in range(cols):

            @pl.when(index == k)
            def _(piece=piece, k=k):
                qkv_out[:, k * width : (k + 1) * width] = piece[:feats, :width].astype(F32)

        out_out[part(index, high), :] = piece[:feats, width:].astype(F32).T
        tail = piece[feats:, :bias].astype(F32)
        bias_out[:, part(index, bias)] = tail[0:1] + tail[1:2]


def first_back_kernel(place, keep, recv, normed, rstd, vec, resid, sums, own, *refs):
    sends, total = refs[:-1], refs[-1]
    cols = len(sends) + 1
    feats = own.shape[1]
    extent, width = keep.shape
    grad = keep[...] + recv[...].astype(F32)
    n = normed[...]
    scaled = grad * vec[0:1]
    one = jnp.sum(scaled, 1, keepdims=True) / width
    two = jnp.sum(scaled * n, 1, keepdims=True) / width
    total[:extent] = rstd[...] * scaled
    mine = part(place[0], resid.shape[0])
    total[mine, :] = total[mine, :] + resid[...]
    gain_sum = jnp.sum(grad * n, 0, keepdims=True)
    shift_sum = jnp.sum(grad, 0, keepdims=True)
    lane = lax.broadcasted_iota(jnp.int32, (extent, 128), 1)
    stats = jnp.where(lane == 0, one, jnp.where(lane == 1, two, 0.0)).T[:2]
    stats = jnp.concatenate([stats, jnp.zeros((2, feats - extent), F32)], 1)
    tail = total.at[extent : extent + 8]
    tail[0:4] = sums[0:4]
    tail[4:5] = gain_sum
    tail[5:6] = shift_sum
    for step, out in enumerate((own, *sends)):
        at = part(target(place, step, cols), feats)
        out[:extent] = total[:extent, at].astype(out.dtype)
        ends = jnp.concatenate([tail[0:6, at], stats], 0)
        high, low = split_rows(ends)
        out[extent:] = jnp.concatenate([high.astype(F32), low.astype(F32)], 0).astype(out.dtype)


def tokens_final_kernel(place, normed, rstd, own, *refs):
    received, (out, sums) = refs[:-2], refs[-2:]
    extent, feats = out.shape
    total = total_of(own, received)
    ends = total[extent : extent + 8] + total[extent + 8 : extent + 16]
    sums[...] = ends
    lanes = jnp.concatenate([ends[6:8, :extent], jnp.zeros((6, extent), F32)], 0)
    square = jnp.concatenate([lanes, jnp.zeros((120, extent), F32)], 0).T
    n = normed[:, part(place[0], feats)]
    out[...] = total[:extent] - rstd[...] * (square[:, 0:1] + n * square[:, 1:2])


def scatter_row(keep, send, place):
    bit = 1
    while bit < lax.axis_size("row") // 2:
        recv = swap(send, "row", bit)
        half = (keep.shape[0] // 2, keep.shape[1])
        keep, send = call(fold_kernel, [(half, F32), (half, BF16)], place, keep, recv)
        bit *= 2
    return (keep, swap(send, "row", bit))


def local(
    tokens,
    cotangent,
    first_gain,
    first_shift,
    w_qkv,
    bias_qv,
    w_out,
    bias_out,
    second_gain,
    second_shift,
    w_up,
    bias_up,
    w_down,
    bias_down,
):
    cols = lax.axis_size("col")
    rows = lax.axis_size("row")
    own_col = lax.axis_index("col")
    own_row = lax.axis_index("row")
    place = jnp.stack([own_col, own_row]).astype(jnp.int32)
    extent, feats = tokens.shape
    width = feats * cols
    group = extent * rows
    half = group // 2
    count = extent // cols
    head_count = bias_qv.shape[0] // (2 * HEAD_DIM)
    heads = head_count // cols
    qkv_cols = w_qkv.shape[1] // cols
    ff_cols = w_up.shape[1] // cols
    out_rows = w_out.shape[0] // cols
    order = block_order(rows)
    head_ids = own_row * head_count + own_col * heads + jnp.arange(heads, dtype=jnp.int32)
    slopes = jnp.exp2(-8.0 * (head_ids.astype(F32) + 1.0) / HEADS)

    vectors = [first_gain, first_shift, bias_out, second_gain, second_shift]
    vectors = jnp.stack(vectors + [jnp.zeros_like(first_gain)] * (8 - len(vectors)))
    head_block = pl.pallas_call(
        head_kernel,
        out_shape=jax.ShapeDtypeStruct((extent + PAD, feats), BF16),
        in_specs=[VM, VM],
        out_specs=VM,
        compiler_params=pltpu.CompilerParams(vmem_limit_bytes=GRANT),
        name="head",
    )(tokens, vectors)
    heads_in = exchange([head_block] * cols)
    qkv_blocks = call(
        qkv_pieces_kernel,
        [((feats, qkv_cols + out_rows), BF16)] * cols,
        place,
        w_qkv,
        w_out,
        hbm=(0, 1),
        scratch=[
            pltpu.VMEM(w_qkv.shape, BF16),
            pltpu.VMEM(w_out.shape, BF16),
            pltpu.SemaphoreType.DMA((2,)),
        ],
    )
    qkv_in = exchange(qkv_blocks)
    first_in, normed_one, rstd_one, x_rows, vec = call(
        first_norm_kernel,
        [
            ((extent, width), BF16),
            ((extent, width), F32),
            ((extent, 1), F32),
            ((extent, width), BF16),
            ((8, width), F32),
        ],
        place,
        *heads_in,
    )
    first_all = gather_row(first_in)

    cot_late, up_late, down_late = lax.optimization_barrier(
        (cotangent, w_up, w_down, first_in)
    )[:3]
    ff_blocks = call(
        ff_pieces_kernel,
        [((feats + ff_cols + extent, feats), BF16)] * cols,
        place,
        cot_late,
        up_late,
        down_late,
        hbm=(0, 1, 2),
        scratch=[pltpu.SemaphoreType.DMA((3 * cols,))],
    )
    ff_in = exchange(ff_blocks)

    wide = (group, heads * HEAD_DIM)
    partial_outs = [((half, width), F32), ((half, width), BF16)]
    body = functools.partial(attention_kernel, order, heads, cols)

    def attention_body(place_ref, slopes_ref, *refs):
        body(place_ref, slopes_ref, *refs)

    q, k, v, logs, context, wq, wo, keep, send = call_slopes(
        attention_body,
        [
            (wide, BF16),
            (wide, BF16),
            (wide, BF16),
            ((group, heads), F32),
            (wide, BF16),
            ((width, qkv_cols), BF16),
            ((width, out_rows), BF16),
        ]
        + partial_outs,
        place,
        slopes,
        bias_qv.reshape(1, -1),
        *first_all,
        *qkv_in,
    )
    keep, recv = scatter_row(keep, send, place)
    own, *sends = call(
        to_tokens_kernel,
        [((count, width), F32)] + [((count, width), BF16)] * (cols - 1),
        place,
        keep,
        recv,
    )
    received = exchange([own, *sends])[1:]
    resid, normed_two, rstd_two, second_in = call(
        second_norm_kernel,
        [
            ((count, width), F32),
            ((count, width), F32),
            ((count, 1), F32),
            ((count, width), BF16),
        ],
        place,
        own,
        *received,
        x_rows,
        vec,
    )
    (second_rows,) = call(
        join_rows_kernel, [((extent, width), BF16)], place, *exchange([second_in] * cols)
    )
    second_all = gather_row(second_rows)

    w_up_s, w_down_s, cot_rows = call(
        ff_join_kernel,
        [((width, ff_cols), BF16), ((ff_cols, width), BF16), ((extent, width), BF16)],
        place,
        *ff_in,
    )
    cot_all = gather_row(cot_rows)
    (cot_down,) = call(
        cot_kernel,
        [((group, ff_cols), F32)],
        place,
        w_down_s,
        *cot_all,
        flops=2 * group * width * ff_cols,
    )
    (probs,) = call_slopes(
        functools.partial(probs_kernel, order, heads),
        [((heads, group, group), F32)],
        place,
        slopes,
        q,
        k,
        logs,
    )

    act, grad_pre, up_bias_part, keep, send = call(
        hidden_kernel,
        [((group, ff_cols), BF16), ((group, ff_cols), BF16), ((1, ff_cols), F32)] + partial_outs,
        place,
        w_up_s,
        bias_up.reshape(1, -1),
        cot_down,
        *second_all,
        flops=4 * group * width * ff_cols,
    )
    keep, recv = scatter_row(keep, send, place)
    own, *sends = call(
        to_tokens_kernel,
        [((count, width), F32)] + [((count, width), BF16)] * (cols - 1),
        place,
        keep,
        recv,
    )
    received = exchange([own, *sends])[1:]
    grad_resid, resid_b, sums = call(
        second_back_kernel,
        [((count, width), F32), ((count, width), BF16), ((8, width), F32)],
        place,
        own,
        *received,
        normed_two,
        rstd_two,
        vec,
        cot_rows,
    )
    (resid_rows,) = call(
        join_rows_kernel, [((extent, width), BF16)], place, *exchange([resid_b] * cols)
    )
    resid_all = gather_row(resid_rows)

    keep, send = call(
        out_part_kernel, partial_outs, place, act, w_down_s, flops=2 * group * width * ff_cols
    )
    keep, recv = scatter_row(keep, send, place)
    own, *sends = call(
        out_features_kernel,
        [((extent, feats), F32)] + [((extent, feats), BF16)] * (cols - 1),
        place,
        keep,
        recv,
        resid,
        scratch=[pltpu.VMEM((extent, width), F32)],
    )
    (block_out,) = call(
        block_out_kernel,
        [((extent, feats), BF16)],
        place,
        bias_down.reshape(1, -1),
        own,
        *exchange([own, *sends])[1:],
    )

    (ff_message,) = call(
        functools.partial(ff_grad_kernel, rows, cols),
        [((cols * (feats + ff_cols) + PAD, ff_cols), BF16)],
        place,
        act,
        grad_pre,
        up_bias_part,
        *second_all,
        *cot_all,
        flops=4 * group * width * ff_cols,
    )
    ff_shape = (feats + ff_cols + PAD, ff_cols)
    ff_sums = call(
        dp_sum_kernel,
        [(ff_shape, F32)] + [(ff_shape, BF16)] * (cols - 1),
        place,
        *swap_dp(ff_message),
    )
    grad_w_up, grad_w_down, grad_bias_up = call(
        ff_final_kernel,
        [(w_up.shape, F32), (w_down.shape, F32), ((1, bias_up.shape[0]), F32)],
        place,
        *exchange(ff_sums),
    )

    joined, qv_bias_part, keep, send = call(
        functools.partial(attention_back_kernel, rows, heads),
        [((group, qkv_cols), BF16), ((1, 2 * heads * HEAD_DIM), F32)] + partial_outs,
        place,
        wq,
        wo,
        q,
        k,
        v,
        context,
        probs,
        *resid_all,
        scratch=[pltpu.VMEM(wide, BF16)],
    )
    (qkv_message,) = call(
        functools.partial(qkv_grad_kernel, rows),
        [((width + PAD, qkv_cols + out_rows), BF16)],
        place,
        joined,
        context,
        qv_bias_part,
        *first_all,
        *resid_all,
        flops=2 * group * width * (qkv_cols + out_rows),
    )
    qkv_shape = (feats + PAD, qkv_cols + out_rows)
    qkv_sums = call(
        dp_sum_kernel,
        [(qkv_shape, F32)] + [(qkv_shape, BF16)] * (cols - 1),
        place,
        *swap_dp(qkv_message),
    )
    grad_w_qkv, grad_w_out, grad_bias_qv = call(
        qkv_final_kernel,
        [(w_qkv.shape, F32), (w_out.shape, F32), ((1, bias_qv.shape[0]), F32)],
        place,
        *exchange(qkv_sums),
    )

    keep, recv = scatter_row(keep, send, place)
    last_shape = (extent + PAD, feats)
    last = call(
        first_back_kernel,
        [(last_shape, F32)] + [(last_shape, BF16)] * (cols - 1),
        place,
        keep,
        recv,
        normed_one,
        rstd_one,
        vec,
        grad_resid,
        sums,
        scratch=[pltpu.VMEM((extent + 8, width), F32)],
    )
    grad_tokens, col_sums = call(
        tokens_final_kernel,
        [((extent, feats), F32), ((8, feats), F32)],
        place,
        normed_one,
        rstd_one,
        *exchange(last),
    )
    col_sums = sum_small(sum_small(col_sums, "row"), "dp")

    return (
        block_out,
        grad_tokens,
        col_sums[4],
        col_sums[5],
        grad_w_qkv,
        grad_bias_qv.reshape(-1),
        grad_w_out,
        col_sums[2],
        col_sums[0],
        col_sums[1],
        grad_w_up,
        grad_bias_up.reshape(-1),
        grad_w_down,
        col_sums[3],
    )


def call_slopes(body, outs, place, slopes, *args):
    shapes = [jax.ShapeDtypeStruct(shape, kind) for shape, kind in outs]
    moved = sum(a.size * a.dtype.itemsize for a in args)
    moved += sum(s.size * s.dtype.itemsize for s in shapes)
    return pl.pallas_call(
        body,
        out_shape=shapes,
        in_specs=[SM, SM] + [VM] * len(args),
        out_specs=[VM] * len(shapes),
        compiler_params=pltpu.CompilerParams(vmem_limit_bytes=GRANT),
        cost_estimate=pl.CostEstimate(flops=1 << 31, bytes_accessed=moved, transcendentals=1 << 19),
    )(place, slopes, *args)


def solution(mesh):
    tokens_spec = P(("dp", "row"), "col")
    vector = P("col")
    placed = (
        tokens_spec,
        tokens_spec,
        vector,
        vector,
        P("col", "row"),
        P("row"),
        P("row", "col"),
        vector,
        vector,
        vector,
        P("col", "row"),
        P("row"),
        P("row", "col"),
        vector,
    )


    return jax.shard_map(
        local,
        mesh=mesh,
        in_specs=placed,
        out_specs=(
            tokens_spec,
            tokens_spec,
            vector,
            vector,
            P("col", "row"),
            P("row"),
            P("row", "col"),
            vector,
            vector,
            vector,
            P("col", "row"),
            P("row"),
            P("row", "col"),
            vector,
        ),
        check_vma=False,
    )
```

```python
import functools

import jax
import jax.numpy as jnp
from jax import lax
from jax.experimental import pallas as pl
from jax.experimental.pallas import tpu as pltpu
from jax.sharding import PartitionSpec as P


HEADS = 16
HEAD_DIM = 64
SEQ = 512

EPS = 1e-05
GELU_C = 0.7978845608028654
GELU_A = 0.044715
BF16 = jnp.bfloat16
F32 = jnp.float32
PAD = 16
GRANT = 12 << 20


VM = pl.BlockSpec(memory_space=pltpu.VMEM)
SM = pl.BlockSpec(memory_space=pltpu.SMEM)
HB = pl.BlockSpec(memory_space=pltpu.HBM)


def call(body, outs, place, *args, flops=0, scratch=(), hbm=()):
    shapes = [jax.ShapeDtypeStruct(shape, kind) for shape, kind in outs]
    moved = sum(a.size * a.dtype.itemsize for a in args)
    moved += sum(s.size * s.dtype.itemsize for s in shapes)
    return pl.pallas_call(
        body,
        out_shape=shapes,
        in_specs=[SM] + [HB if i in hbm else VM for i in range(len(args))],
        out_specs=[VM] * len(shapes),
        scratch_shapes=list(scratch),
        compiler_params=pltpu.CompilerParams(vmem_limit_bytes=GRANT),
        cost_estimate=pl.CostEstimate(flops=flops, bytes_accessed=moved, transcendentals=0),
    )(place, *args)


def mm(left, right, left_dim, right_dim):
    return lax.dot_general(
        left, right, (((left_dim,), (right_dim,)), ((), ())), preferred_element_type=F32
    )


def part(index, extent):
    return pl.ds(pl.multiple_of(index * extent, extent), extent)


def source(place, step, cols):
    return lax.rem(place[0] + cols - step, cols)


def target(place, step, cols):
    return lax.rem(place[0] + step, cols)


def split_rows(values):
    high = values.astype(BF16)
    return (high, (values - high.astype(F32)).astype(BF16))


def block_order(rows):
    order = [0]
    bit = rows // 2
    while bit:
        order = order + [o ^ bit for o in order]
        bit //= 2
    return order


def positions(place, order, extent, axis):
    shape = (extent, 1) if axis == 0 else (1, extent)
    pieces = [
        lax.broadcasted_iota(jnp.int32, shape, axis) + jnp.bitwise_xor(place[1], o) * extent
        for o in order
    ]
    return pieces if axis == 0 else jnp.concatenate(pieces, axis)


def shift(block, axis, step):
    size = lax.axis_size(axis)
    return lax.ppermute(block, axis, [(i, (i + step) % size) for i in range(size)])


def swap(block, axis, bit):
    size = lax.axis_size(axis)
    return lax.ppermute(block, axis, [(i, i ^ bit) for i in range(size)])


def exchange(blocks):
    return [blocks[0]] + [shift(blocks[s], "col", s) for s in range(1, len(blocks))]


def gather_row(block):
    pieces = [block]
    bit = lax.axis_size("row") // 2
    while bit:
        for i in range(len(pieces)):
            pieces = pieces + [swap(pieces[i], "row", bit)]
        bit //= 2
    return pieces


def sum_small(small, axis):
    bit = 1
    while bit < lax.axis_size(axis):
        other = swap(small, axis, bit)
        small = small + other
        bit *= 2
    return small


def swap_dp(block):
    return swap(block, "dp", 1)


def sum_rest(keep, recv):
    size = lax.axis_size("dp")
    bit = 2
    while bit < size:
        keep = (keep.astype(F32) + recv.astype(F32)).astype(BF16)
        recv = swap(keep, "dp", bit)
        bit *= 2
    return (keep, recv)


def head_kernel(tokens, vectors, out):
    rows = tokens.shape[0]
    out[:rows] = tokens[...]
    high, low = split_rows(vectors[...])
    out[rows:] = jnp.concatenate([high.astype(F32), low.astype(F32)], 0).astype(BF16)


def qkv_pieces_kernel(place, w_qkv_hbm, w_out_hbm, *refs):
    outs, (w_qkv, w_out, sems) = refs[:-3], refs[-3:]
    copies = [
        pltpu.make_async_copy(w_qkv_hbm, w_qkv, sems.at[0]),
        pltpu.make_async_copy(w_out_hbm, w_out, sems.at[1]),
    ]
    for copy in copies:
        copy.start()
    for copy in copies:
        copy.wait()
    cols = len(outs)
    width = w_qkv.shape[1] // cols
    height = w_out.shape[0] // cols
    for step, out in enumerate(outs):
        for k in range(cols):

            @pl.when(target(place, step, cols) == k)
            def _(out=out, k=k):
                out[:, :width] = w_qkv[:, k * width : (k + 1) * width]
                out[:, width:] = w_out[k * height : (k + 1) * height].astype(F32).T.astype(BF16)


def ff_pieces_kernel(place, w_up, w_down, *refs):
    outs, sems = refs[:-1], refs[-1]
    cols = len(outs)
    width = w_up.shape[1] // cols

    def blocks(of):
        copies = [
            pltpu.make_async_copy(of(target(place, step, cols)), out, sems.at[step])
            for step, out in enumerate(outs)
        ]
        for copy in copies:
            copy.start()
        for copy in copies:
            copy.wait()

    @pl.when(place[2] == 0)
    def _():
        blocks(lambda index: w_up.at[:, part(index, width)])

    @pl.when(place[2] == 1)
    def _():
        blocks(lambda index: w_down.at[part(index, width), :])


def first_norm_kernel(place, *refs):
    cols = len(refs) - 5
    pieces, (first_in, normed_out, rstd_out, x_out, vec_out) = refs[:cols], refs[cols:]
    rows = first_in.shape[0]
    feats = pieces[0].shape[1]
    for step, piece in enumerate(pieces):
        at = part(source(place, step, cols), feats)
        x_out[:, at] = piece[:rows]
        tail = piece[rows:].astype(F32)
        vec_out[:, at] = tail[:8] + tail[8:]
    x = x_out[...].astype(F32)
    width = x.shape[1]
    centre = jnp.sum(x, 1, keepdims=True) / width
    spread = jnp.sum(x * x, 1, keepdims=True) / width - centre * centre
    rstd = lax.rsqrt(spread + EPS)
    normed = (x - centre) * rstd
    normed_out[...] = normed
    rstd_out[...] = rstd
    first_in[...] = (normed * vec_out[0:1] + vec_out[1:2]).astype(BF16)


def attention_kernel(order, heads, cols, place, slopes, bias, *refs):
    rows = len(order)
    first, weights = refs[:rows], refs[rows : rows + cols]
    q_out, k_out, v_out, log_out, ctx_out, wq_out, wo_out, keep, send = refs[rows + cols :]
    feats = weights[0].shape[0]
    width = wq_out.shape[1]
    for step, piece in enumerate(weights):
        at = part(source(place, step, cols), feats)
        wq_out[at, :] = piece[:, :width]
        wo_out[at, :] = piece[:, width:]
    extent = first[0].shape[0]
    own_bias = bias[:, part(place[0], 2 * heads * HEAD_DIM)]
    for p in range(rows):
        joined = mm(first[p][...], wq_out[...], 1, 0)
        at = slice(p * extent, (p + 1) * extent)
        for h in range(heads):
            here = slice(h * HEAD_DIM, (h + 1) * HEAD_DIM)
            base = 3 * h * HEAD_DIM
            b = 2 * h * HEAD_DIM
            q = joined[:, base : base + HEAD_DIM] + own_bias[:, b : b + HEAD_DIM]
            v = joined[:, base + 2 * HEAD_DIM : base + 3 * HEAD_DIM]
            v = v + own_bias[:, b + HEAD_DIM : b + 2 * HEAD_DIM]
            q_out[at, here] = q.astype(BF16)
            k_out[at, here] = joined[:, base + HEAD_DIM : base + 2 * HEAD_DIM].astype(BF16)
            v_out[at, here] = v.astype(BF16)
    for p in range(rows):
        at = slice(p * extent, (p + 1) * extent)
        for h in range(heads):
            here = slice(h * HEAD_DIM, (h + 1) * HEAD_DIM)
            scores = block_scores(place, order, extent, p, q_out[at, here], k_out[:, here], slopes[h])
            expo = jnp.exp(scores)
            total = jnp.sum(expo, 1, keepdims=True)
            log_out[at, h : h + 1] = jnp.log(total)
            numerator = mm(expo.astype(BF16), v_out[:, here], 1, 0)
            ctx_out[at, here] = (numerator / total).astype(BF16)
    half = keep.shape[0]
    keep[...] = mm(ctx_out[:half], wo_out[...], 1, 1)
    send[...] = mm(ctx_out[half:], wo_out[...], 1, 1).astype(BF16)


def block_scores(place, order, extent, p, query, keys, slope):
    query_pos = positions(place, order[p : p + 1], extent, 0)[0]
    key_pos = positions(place, order, extent, 1)
    offsets = query_pos - key_pos
    same = lax.div(query_pos, jnp.int32(SEQ)) == lax.div(key_pos, jnp.int32(SEQ))
    scores = mm(query, keys, 1, 1) * 0.125 - slope * offsets.astype(F32)
    return jnp.where((offsets >= 0) & same, scores, -30000.0)


def probs_kernel(order, heads, place, slopes, q, k, logs, out):
    rows = len(order)
    extent = q.shape[0] // rows
    for h in range(heads):
        here = slice(h * HEAD_DIM, (h + 1) * HEAD_DIM)
        for p in range(rows):
            at = slice(p * extent, (p + 1) * extent)
            scores = block_scores(place, order, extent, p, q[at, here], k[:, here], slopes[h])
            out[h, at, :] = jnp.exp(scores - logs[at, h : h + 1])


def fold_kernel(place, keep, recv, keep_out, send_out):
    half = keep_out.shape[0]
    keep_out[...] = keep[:half] + recv[:half].astype(F32)
    send_out[...] = (keep[half:] + recv[half:].astype(F32)).astype(BF16)


def to_tokens_kernel(place, keep, recv, own, *sends):
    cols = len(sends) + 1
    count = own.shape[0]
    for step, out in enumerate((own, *sends)):
        at = part(target(place, step, cols), count)
        out[...] = (keep[at, :] + recv[at, :].astype(F32)).astype(out.dtype)


def total_of(own, received):
    total = own[...]
    for piece in received:
        total = total + piece[...].astype(F32)
    return total


def second_norm_kernel(place, own, *refs):
    received, (x, vec, resid_out, normed_out, rstd_out, second_in) = refs[:-6], refs[-6:]
    count = own.shape[0]
    x_own = x[part(place[0], count), :].astype(F32)
    resid = x_own + total_of(own, received) + vec[2:3]
    width = resid.shape[1]
    centre = jnp.sum(resid, 1, keepdims=True) / width
    spread = jnp.sum(resid * resid, 1, keepdims=True) / width - centre * centre
    rstd = lax.rsqrt(spread + EPS)
    normed = (resid - centre) * rstd
    resid_out[...] = resid
    normed_out[...] = normed
    rstd_out[...] = rstd
    second_in[...] = (normed * vec[3:4] + vec[4:5]).astype(BF16)


def join_rows_kernel(place, *refs):
    pieces, out = refs[:-1], refs[-1]
    count = pieces[0].shape[0]
    for step, piece in enumerate(pieces):
        out[part(source(place, step, len(pieces)), count), :] = piece[...]


def ff_join_kernel(place, *refs):
    pieces, half_out = refs[:-1], refs[-1]
    cols = len(pieces)
    width = half_out.shape[0] // cols
    for step, piece in enumerate(pieces):
        half_out[part(source(place, step, cols), width), :] = piece[...]


def join_lanes_kernel(place, *refs):
    pieces, out = refs[:-1], refs[-1]
    feats = pieces[0].shape[1]
    for step, piece in enumerate(pieces):
        out[:, part(source(place, step, len(pieces)), feats)] = piece[...]


def cat_kernel(place, *refs):
    pieces, out = refs[:-1], refs[-1]
    extent = pieces[0].shape[0]
    for p, piece in enumerate(pieces):
        out[p * extent : (p + 1) * extent] = piece[...]


def cot_kernel(cols, place, mine, other, *refs):
    pieces, (out, up_out, down_out) = refs[:-3], refs[-3:]
    extent, width = pieces[0].shape

    @pl.when(place[2] == 0)
    def _():
        up_out[...] = mine[...]
        down_out[...] = other[...]

    @pl.when(place[2] == 1)
    def _():
        up_out[...] = other[...]
        down_out[...] = mine[...]

    feats = width // cols
    height = down_out.shape[0] // cols
    for p, piece in enumerate(pieces):
        total = jnp.zeros((extent, height), F32)
        for j in range(cols):
            block = down_out[j * height : (j + 1) * height]
            total = total + mm(piece[:, j * feats : (j + 1) * feats], block, 1, 1)
        out[p * extent : (p + 1) * extent] = total


def hidden_kernel(place, up, bias, cot_down, *refs):
    pieces, (act_out, grad_out, bias_out, keep, send) = refs[:-5], refs[-5:]
    extent = pieces[0].shape[0]
    width = up.shape[1]
    own_bias = bias[:, part(place[0], width)]
    bias_total = jnp.zeros((1, width), F32)
    for p, piece in enumerate(pieces):
        at = slice(p * extent, (p + 1) * extent)
        hidden = mm(piece[...], up[...], 1, 0) + own_bias
        inner = GELU_C * (hidden + GELU_A * hidden * hidden * hidden)
        tanh_val = jnp.tanh(inner)
        act_out[at] = (0.5 * hidden * (1.0 + tanh_val)).astype(BF16)
        slope = 0.5 * (1.0 + tanh_val) + 0.5 * hidden * (1.0 - tanh_val * tanh_val) * GELU_C * (
            1.0 + 3.0 * GELU_A * hidden * hidden
        )
        grad_pre = cot_down[at] * slope
        bias_total = bias_total + jnp.sum(grad_pre, 0, keepdims=True)
        grad_out[at] = grad_pre.astype(BF16)
    bias_out[...] = bias_total
    half = keep.shape[0]
    keep[...] = mm(grad_out[:half], up[...], 1, 1)
    send[...] = mm(grad_out[half:], up[...], 1, 1).astype(BF16)


def out_part_kernel(cols, place, act, down, keep, send):
    half, width = keep.shape
    feats = width // cols
    height = down.shape[0] // cols
    for j in range(cols):
        here = slice(j * feats, (j + 1) * feats)
        block = down[j * height : (j + 1) * height]
        keep[:, here] = mm(act[:half], block, 1, 0)
        send[:, here] = mm(act[half:], block, 1, 0).astype(BF16)


def out_features_kernel(place, keep, recv, resid, own, *refs):
    sends, total = refs[:-1], refs[-1]
    cols = len(sends) + 1
    feats = own.shape[1]
    total[...] = keep[...] + recv[...].astype(F32)
    mine = part(place[0], resid.shape[0])
    total[mine, :] = total[mine, :] + resid[...]
    for step, out in enumerate((own, *sends)):
        out[...] = total[:, part(target(place, step, cols), feats)].astype(out.dtype)


def block_out_kernel(place, bias, own, *refs):
    received, out = refs[:-1], refs[-1]
    out[...] = (total_of(own, received) + bias[...]).astype(BF16)


def ff_grad_kernel(rows, cols, place, act, grad, bias, *refs):
    second, cots, (keep, send) = refs[:rows], refs[rows : 2 * rows], refs[2 * rows :]
    extent = second[0].shape[0]
    feats = second[0].shape[1] // cols
    width = grad.shape[1]
    for j in range(cols):
        here = slice(j * feats, (j + 1) * feats)
        up = jnp.zeros((feats, width), F32)
        down = jnp.zeros((width, feats), F32)
        for p in range(rows):
            at = slice(p * extent, (p + 1) * extent)
            up = up + mm(second[p][:, here], grad[at], 0, 0)
            down = down + mm(act[at], cots[p][:, here], 0, 0)
        there = slice(j * width, (j + 1) * width)
        even = place[2] == 0
        keep[there] = jnp.where(even, up, down)
        send[there] = jnp.where(even, down, up).astype(BF16)
    ends = pair_rows(bias[...])
    keep[cols * width :] = ends.astype(F32)
    send[cols * width :] = ends


def pair_rows(vector):
    high, low = split_rows(vector)
    empty = jnp.zeros((PAD - 2, vector.shape[1]), F32)
    return jnp.concatenate([high.astype(F32), low.astype(F32), empty], 0).astype(BF16)


def dp_sum_kernel(place, mine, other, own, *sends):
    cols = len(sends) + 1
    stride = own.shape[0] - PAD
    tail = cols * stride
    ends = mine[tail:].astype(F32) + other[tail:].astype(F32)
    both = ends[0:1] + ends[1:2]
    for step, out in enumerate((own, *sends)):
        at = part(target(place, step, cols), stride)
        out[:stride] = (mine[at, :].astype(F32) + other[at, :].astype(F32)).astype(out.dtype)
        out[stride:] = pair_rows(both).astype(out.dtype)


def half_join_kernel(place, *refs):
    pieces, (half_out, bias_out) = refs[:-2], refs[-2:]
    cols = len(pieces)
    width = half_out.shape[0] // cols
    for step, piece in enumerate(pieces):
        index = source(place, step, cols)
        half_out[part(index, width), :] = piece[:width]
        tail = piece[width:].astype(F32)
        bias_out[:, part(index, width)] = tail[0:1] + tail[1:2]


def ff_final_kernel(place, mine, other, up_out, down_out):
    def write(up, down):
        width = up.shape[1]
        for k in range(up.shape[0] // width):
            here = slice(k * width, (k + 1) * width)
            up_out[:, here] = up[here].astype(F32)
        down_out[...] = down[...].astype(F32)

    @pl.when(place[2] == 0)
    def _():
        write(mine, other)

    @pl.when(place[2] == 1)
    def _():
        write(other, mine)


def second_back_kernel(place, own, *refs):
    received = refs[:-7]
    normed, rstd, vec, cot, resid_out, resid_b, sums = refs[-7:]
    count = own.shape[0]
    grad = total_of(own, received)
    n = normed[...]
    width = grad.shape[1]
    scaled = grad * vec[3:4]
    mean_one = jnp.sum(scaled, 1, keepdims=True) / width
    mean_two = jnp.sum(scaled * n, 1, keepdims=True) / width
    cot_own = cot[part(place[0], count), :].astype(F32)
    resid = cot_own + rstd[...] * (scaled - mean_one - n * mean_two)
    resid_out[...] = resid
    resid_b[...] = resid.astype(BF16)
    sums[0:1] = jnp.sum(grad * n, 0, keepdims=True)
    sums[1:2] = jnp.sum(grad, 0, keepdims=True)
    sums[2:3] = jnp.sum(resid, 0, keepdims=True)
    sums[3:4] = jnp.sum(cot_own, 0, keepdims=True)
    sums[4:8] = jnp.zeros((4, width), F32)


def attention_back_kernel(rows, heads, place, wq, wo, q, k, v, ctx, probs, *refs):
    resid = refs[:rows]
    joined_out, keep, send, gctx, bias_out = refs[rows:]
    size = q.shape[0]
    extent = resid[0].shape[0]
    for p in range(rows):
        at = slice(p * extent, (p + 1) * extent)
        gctx[at] = mm(resid[p][...], wo[...], 1, 0).astype(BF16)
    for h in range(heads):
        here = slice(h * HEAD_DIM, (h + 1) * HEAD_DIM)
        base = 3 * h * HEAD_DIM
        grad_k = jnp.zeros((size, HEAD_DIM), F32)
        grad_v = jnp.zeros((size, HEAD_DIM), F32)
        bias_q = jnp.zeros((1, HEAD_DIM), F32)
        for p in range(rows):
            at = slice(p * extent, (p + 1) * extent)
            grad = gctx[at, here]
            delta = jnp.sum(grad.astype(F32) * ctx[at, here].astype(F32), 1, keepdims=True)
            prob = probs[h, at, :]
            dscore = (prob * (mm(grad, v[:, here], 1, 1) - delta)).astype(BF16)
            grad_q = mm(dscore, k[:, here], 1, 0) * 0.125
            bias_q = bias_q + jnp.sum(grad_q, 0, keepdims=True)
            joined_out[at, base : base + HEAD_DIM] = grad_q.astype(BF16)
            grad_k = grad_k + mm(dscore, q[at, here], 0, 0)
            grad_v = grad_v + mm(prob.astype(BF16), grad, 0, 0)
        joined_out[:size, base + HEAD_DIM : base + 2 * HEAD_DIM] = (grad_k * 0.125).astype(BF16)
        joined_out[:size, base + 2 * HEAD_DIM : base + 3 * HEAD_DIM] = grad_v.astype(BF16)
        b = 2 * h * HEAD_DIM
        bias_out[:, b : b + HEAD_DIM] = bias_q
        bias_out[:, b + HEAD_DIM : b + 2 * HEAD_DIM] = jnp.sum(grad_v, 0, keepdims=True)
    rest = joined_out.shape[1] - bias_out.shape[1]
    joined_out[size:] = pair_rows(
        jnp.concatenate([bias_out[...], jnp.zeros((1, rest), F32)], 1)
    )
    half = keep.shape[0]
    keep[...] = mm(joined_out[:half], wq[...], 1, 1)
    send[...] = mm(joined_out[half:size], wq[...], 1, 1).astype(BF16)


def out_grad_kernel(rows, place, ctx, *refs):
    resid, out = refs[:rows], refs[-1]
    extent = resid[0].shape[0]
    total = jnp.zeros(out.shape, F32)
    for p in range(rows):
        total = total + mm(ctx[p * extent : (p + 1) * extent], resid[p][...], 0, 0)
    out[...] = total.astype(BF16)


def qkv_own_kernel(rows, place, joined, *refs):
    first, out = refs[:rows], refs[-1]
    extent = first[0].shape[0]
    grad = jnp.zeros(out.shape, F32)
    for p in range(rows):
        grad = grad + mm(first[p][...], joined[p * extent : (p + 1) * extent], 0, 0)
    out[...] = grad


def qkv_sum_kernel(rows, bias, place, mine, joined, peer, peer_first, out_a, out_b, *refs):
    outs, whole = refs[:-1], refs[-1]
    cols = len(outs)
    high, width = mine.shape
    size = joined.shape[0] - PAD
    extent = size // rows
    grad = jnp.zeros(mine.shape, F32)
    for p in range(rows):
        at = slice(p * extent, (p + 1) * extent)
        grad = grad + mm(peer_first[at], peer[at], 0, 0)
    whole[:high, :width] = mine[...] + grad
    whole[:high, width:] = (out_a[...].astype(F32) + out_b[...].astype(F32)).T
    ends = joined[size:].astype(F32) + peer[size:].astype(F32)
    ends = ends[0:1, :bias] + ends[1:2, :bias]
    ends = jnp.concatenate([ends, jnp.zeros((1, whole.shape[1] - bias), F32)], 1)
    if cols == 1:
        outs[0][:high] = whole[...].astype(BF16)
        outs[0][high:] = pair_rows(ends)
        return
    stride = high // cols
    for step, out in enumerate(outs):
        at = part(target(place, step, cols), stride)
        out[:stride] = whole[at, :].astype(out.dtype)
        out[stride:] = pair_rows(ends).astype(out.dtype)


def qkv_final_kernel(place, *refs):
    pieces, (qkv_out, out_out, bias_out) = refs[:-3], refs[-3:]
    cols = len(pieces)
    feats = qkv_out.shape[0]
    width = qkv_out.shape[1] // cols
    high = out_out.shape[0] // cols
    bias = bias_out.shape[1] // cols
    for step, piece in enumerate(pieces):
        index = source(place, step, cols)
        for k in range(cols):

            @pl.when(index == k)
            def _(piece=piece, k=k):
                qkv_out[:, k * width : (k + 1) * width] = piece[:feats, :width].astype(F32)

        out_out[part(index, high), :] = piece[:feats, width:].astype(F32).T
        tail = piece[feats:, :bias].astype(F32)
        bias_out[:, part(index, bias)] = tail[0:1] + tail[1:2]


def first_back_kernel(place, keep, recv, normed, rstd, vec, resid, sums, own, *refs):
    sends, total = refs[:-1], refs[-1]
    cols = len(sends) + 1
    feats = own.shape[1]
    extent, width = keep.shape
    grad = keep[...] + recv[...].astype(F32)
    n = normed[...]
    scaled = grad * vec[0:1]
    one = jnp.sum(scaled, 1, keepdims=True) / width
    two = jnp.sum(scaled * n, 1, keepdims=True) / width
    total[:extent] = rstd[...] * scaled
    mine = part(place[0], resid.shape[0])
    total[mine, :] = total[mine, :] + resid[...]
    gain_sum = jnp.sum(grad * n, 0, keepdims=True)
    shift_sum = jnp.sum(grad, 0, keepdims=True)
    lane = lax.broadcasted_iota(jnp.int32, (extent, 128), 1)
    stats = jnp.where(lane == 0, one, jnp.where(lane == 1, two, 0.0)).T[:2]
    stats = jnp.concatenate([stats, jnp.zeros((2, feats - extent), F32)], 1)
    tail = total.at[extent : extent + 8]
    tail[0:4] = sums[0:4]
    tail[4:5] = gain_sum
    tail[5:6] = shift_sum
    for step, out in enumerate((own, *sends)):
        at = part(target(place, step, cols), feats)
        out[:extent] = total[:extent, at].astype(out.dtype)
        ends = jnp.concatenate([tail[0:6, at], stats], 0)
        high, low = split_rows(ends)
        out[extent:] = jnp.concatenate([high.astype(F32), low.astype(F32)], 0).astype(out.dtype)


def tokens_final_kernel(place, normed, rstd, own, *refs):
    received, (out, sums) = refs[:-2], refs[-2:]
    extent, feats = out.shape
    total = total_of(own, received)
    ends = total[extent : extent + 8] + total[extent + 8 : extent + 16]
    sums[...] = ends
    lanes = jnp.concatenate([ends[6:8, :extent], jnp.zeros((6, extent), F32)], 0)
    square = jnp.concatenate([lanes, jnp.zeros((120, extent), F32)], 0).T
    n = normed[:, part(place[0], feats)]
    out[...] = total[:extent] - rstd[...] * (square[:, 0:1] + n * square[:, 1:2])


def scatter_row(keep, send, place):
    bit = 1
    while bit < lax.axis_size("row") // 2:
        recv = swap(send, "row", bit)
        half = (keep.shape[0] // 2, keep.shape[1])
        keep, send = call(fold_kernel, [(half, F32), (half, BF16)], place, keep, recv)
        bit *= 2
    return (keep, swap(send, "row", bit))


def local(
    tokens,
    cotangent,
    first_gain,
    first_shift,
    w_qkv,
    bias_qv,
    w_out,
    bias_out,
    second_gain,
    second_shift,
    w_up,
    bias_up,
    w_down,
    bias_down,
):
    cols = lax.axis_size("col")
    rows = lax.axis_size("row")
    own_col = lax.axis_index("col")
    own_row = lax.axis_index("row")
    half_id = lax.rem(lax.axis_index("dp"), 2)
    place = jnp.stack([own_col, own_row, half_id]).astype(jnp.int32)
    extent, feats = tokens.shape
    width = feats * cols
    group = extent * rows
    half = group // 2
    count = extent // cols
    head_count = bias_qv.shape[0] // (2 * HEAD_DIM)
    heads = head_count // cols
    qkv_cols = w_qkv.shape[1] // cols
    ff_cols = w_up.shape[1] // cols
    out_rows = w_out.shape[0] // cols
    order = block_order(rows)
    head_ids = own_row * head_count + own_col * heads + jnp.arange(heads, dtype=jnp.int32)
    slopes = jnp.exp2(-8.0 * (head_ids.astype(F32) + 1.0) / HEADS)

    vectors = [first_gain, first_shift, bias_out, second_gain, second_shift]
    vectors = jnp.stack(vectors + [jnp.zeros_like(first_gain)] * (8 - len(vectors)))
    head_block = pl.pallas_call(
        head_kernel,
        out_shape=jax.ShapeDtypeStruct((extent + PAD, feats), BF16),
        in_specs=[VM, VM],
        out_specs=VM,
        compiler_params=pltpu.CompilerParams(vmem_limit_bytes=GRANT),
        name="head",
    )(tokens, vectors)
    heads_in = exchange([head_block] * cols)
    qkv_blocks = call(
        qkv_pieces_kernel,
        [((feats, qkv_cols + out_rows), BF16)] * cols,
        place,
        w_qkv,
        w_out,
        hbm=(0, 1),
        scratch=[
            pltpu.VMEM(w_qkv.shape, BF16),
            pltpu.VMEM(w_out.shape, BF16),
            pltpu.SemaphoreType.DMA((2,)),
        ],
    )
    qkv_in = exchange(qkv_blocks)
    first_in, normed_one, rstd_one, x_rows, vec = call(
        first_norm_kernel,
        [
            ((extent, width), BF16),
            ((extent, width), F32),
            ((extent, 1), F32),
            ((extent, width), BF16),
            ((8, width), F32),
        ],
        place,
        *heads_in,
    )
    first_all = gather_row(first_in)

    up_late, down_late = lax.optimization_barrier((w_up, w_down, first_in))[:2]
    ff_blocks = call(
        ff_pieces_kernel,
        [((ff_cols, feats), BF16)] * cols,
        place,
        up_late,
        down_late,
        hbm=(0, 1),
        scratch=[pltpu.SemaphoreType.DMA((cols,))],
    )
    ff_in = exchange(ff_blocks)

    wide = (group, heads * HEAD_DIM)
    partial_outs = [((half, width), F32), ((half, width), BF16)]
    body = functools.partial(attention_kernel, order, heads, cols)

    def attention_body(place_ref, slopes_ref, *refs):
        body(place_ref, slopes_ref, *refs)

    q, k, v, logs, context, wq, wo, keep, send = call_slopes(
        attention_body,
        [
            (wide, BF16),
            (wide, BF16),
            (wide, BF16),
            ((group, heads), F32),
            (wide, BF16),
            ((width, qkv_cols), BF16),
            ((width, out_rows), BF16),
        ]
        + partial_outs,
        place,
        slopes,
        bias_qv.reshape(1, -1),
        *first_all,
        *qkv_in,
    )
    keep, recv = scatter_row(keep, send, place)
    own, *sends = call(
        to_tokens_kernel,
        [((count, width), F32)] + [((count, width), BF16)] * (cols - 1),
        place,
        keep,
        recv,
    )
    received = exchange([own, *sends])[1:]
    resid, normed_two, rstd_two, second_in = call(
        second_norm_kernel,
        [
            ((count, width), F32),
            ((count, width), F32),
            ((count, 1), F32),
            ((count, width), BF16),
        ],
        place,
        own,
        *received,
        x_rows,
        vec,
    )
    (second_rows,) = call(
        join_rows_kernel, [((extent, width), BF16)], place, *exchange([second_in] * cols)
    )
    second_all = gather_row(second_rows)

    (ff_mine,) = call(ff_join_kernel, [((cols * ff_cols, feats), BF16)], place, *ff_in)
    (cot_rows,) = call(
        join_lanes_kernel, [((extent, width), BF16)], place, *exchange([cotangent] * cols)
    )
    cot_all = gather_row(cot_rows)
    cot_down, w_up_s, w_down_s = call(
        functools.partial(cot_kernel, cols),
        [
            ((group, ff_cols), F32),
            ((cols * ff_cols, feats), BF16),
            ((cols * ff_cols, feats), BF16),
        ],
        place,
        ff_mine,
        swap_dp(ff_mine),
        *cot_all,
        flops=2 * group * width * ff_cols,
    )
    (first_cat,) = call(cat_kernel, [((group, width), BF16)], place, *first_all)
    peer_first = swap_dp(first_cat)
    (probs,) = call_slopes(
        functools.partial(probs_kernel, order, heads),
        [((heads, group, group), F32)],
        place,
        slopes,
        q,
        k,
        logs,
    )

    act, grad_pre, up_bias_part, keep, send = call(
        hidden_kernel,
        [((group, ff_cols), BF16), ((group, ff_cols), BF16), ((1, ff_cols), F32)] + partial_outs,
        place,
        w_up_s,
        bias_up.reshape(1, -1),
        cot_down,
        *second_all,
        flops=4 * group * width * ff_cols,
    )
    keep, recv = scatter_row(keep, send, place)
    own, *sends = call(
        to_tokens_kernel,
        [((count, width), F32)] + [((count, width), BF16)] * (cols - 1),
        place,
        keep,
        recv,
    )
    received = exchange([own, *sends])[1:]
    grad_resid, resid_b, sums = call(
        second_back_kernel,
        [((count, width), F32), ((count, width), BF16), ((8, width), F32)],
        place,
        own,
        *received,
        normed_two,
        rstd_two,
        vec,
        cot_rows,
    )
    (resid_rows,) = call(
        join_rows_kernel, [((extent, width), BF16)], place, *exchange([resid_b] * cols)
    )
    resid_all = gather_row(resid_rows)

    keep, send = call(
        functools.partial(out_part_kernel, cols),
        partial_outs,
        place,
        act,
        w_down_s,
        flops=2 * group * width * ff_cols,
    )
    keep, recv = scatter_row(keep, send, place)
    own, *sends = call(
        out_features_kernel,
        [((extent, feats), F32)] + [((extent, feats), BF16)] * (cols - 1),
        place,
        keep,
        recv,
        resid,
        scratch=[pltpu.VMEM((extent, width), F32)],
    )
    (block_out,) = call(
        block_out_kernel,
        [((extent, feats), BF16)],
        place,
        bias_down.reshape(1, -1),
        own,
        *exchange([own, *sends])[1:],
    )

    ff_shape = (cols * ff_cols + PAD, feats)
    ff_keep, ff_send = call(
        functools.partial(ff_grad_kernel, rows, cols),
        [(ff_shape, F32), (ff_shape, BF16)],
        place,
        act,
        grad_pre,
        up_bias_part,
        *second_all,
        *cot_all,
        flops=4 * group * width * ff_cols,
    )
    ff_sums = call(
        dp_sum_kernel,
        [((ff_cols + PAD, feats), BF16)] * cols,
        place,
        *sum_rest(ff_keep, swap_dp(ff_send)),
    )
    ff_half, grad_bias_up = call(
        half_join_kernel,
        [((cols * ff_cols, feats), BF16), ((1, bias_up.shape[0]), F32)],
        place,
        *exchange(ff_sums),
    )
    grad_w_up, grad_w_down = call(
        ff_final_kernel, [(w_up.shape, F32), (w_down.shape, F32)], place, ff_half, swap_dp(ff_half)
    )

    (out_mine,) = call(
        functools.partial(out_grad_kernel, rows),
        [((out_rows, width), BF16)],
        place,
        context,
        *resid_all,
    )
    joined, keep, send = call(
        functools.partial(attention_back_kernel, rows, heads),
        [((group + PAD, qkv_cols), BF16)] + partial_outs,
        place,
        wq,
        wo,
        q,
        k,
        v,
        context,
        probs,
        *resid_all,
        scratch=[pltpu.VMEM(wide, BF16), pltpu.VMEM((1, 2 * heads * HEAD_DIM), F32)],
    )
    (qkv_mine,) = call(
        functools.partial(qkv_own_kernel, rows),
        [((width, qkv_cols), F32)],
        place,
        joined,
        *first_all,
        flops=2 * group * width * qkv_cols,
    )
    qkv_shape = (feats + PAD, qkv_cols + out_rows)
    single = lax.axis_size("dp") == 2
    whole_shape = (width, qkv_cols + out_rows)
    qkv_sums = call(
        functools.partial(qkv_sum_kernel, rows, 2 * heads * HEAD_DIM),
        [(qkv_shape, F32)] + [(qkv_shape, BF16)] * (cols - 1)
        if single
        else [((width + PAD, qkv_cols + out_rows), BF16)],
        place,
        qkv_mine,
        joined,
        swap_dp(joined),
        peer_first,
        out_mine,
        swap_dp(out_mine),
        scratch=[pltpu.VMEM(whole_shape, F32)],
        flops=2 * group * width * qkv_cols,
    )
    if not single:
        message = qkv_sums[0]
        bit = 2
        while bit < lax.axis_size("dp") // 2:
            message = (message.astype(F32) + swap(message, "dp", bit).astype(F32)).astype(BF16)
            bit *= 2
        qkv_sums = call(
            dp_sum_kernel,
            [(qkv_shape, F32)] + [(qkv_shape, BF16)] * (cols - 1),
            place,
            message,
            swap(message, "dp", bit),
        )
    grad_w_qkv, grad_w_out, grad_bias_qv = call(
        qkv_final_kernel,
        [(w_qkv.shape, F32), (w_out.shape, F32), ((1, bias_qv.shape[0]), F32)],
        place,
        *exchange(qkv_sums),
    )

    keep, recv = scatter_row(keep, send, place)
    last_shape = (extent + PAD, feats)
    last = call(
        first_back_kernel,
        [(last_shape, F32)] + [(last_shape, BF16)] * (cols - 1),
        place,
        keep,
        recv,
        normed_one,
        rstd_one,
        vec,
        grad_resid,
        sums,
        scratch=[pltpu.VMEM((extent + 8, width), F32)],
    )
    grad_tokens, col_sums = call(
        tokens_final_kernel,
        [((extent, feats), F32), ((8, feats), F32)],
        place,
        normed_one,
        rstd_one,
        *exchange(last),
    )
    col_sums = sum_small(sum_small(col_sums, "row"), "dp")

    return (
        block_out,
        grad_tokens,
        col_sums[4],
        col_sums[5],
        grad_w_qkv,
        grad_bias_qv.reshape(-1),
        grad_w_out,
        col_sums[2],
        col_sums[0],
        col_sums[1],
        grad_w_up,
        grad_bias_up.reshape(-1),
        grad_w_down,
        col_sums[3],
    )


def call_slopes(body, outs, place, slopes, *args):
    shapes = [jax.ShapeDtypeStruct(shape, kind) for shape, kind in outs]
    moved = sum(a.size * a.dtype.itemsize for a in args)
    moved += sum(s.size * s.dtype.itemsize for s in shapes)
    return pl.pallas_call(
        body,
        out_shape=shapes,
        in_specs=[SM, SM] + [VM] * len(args),
        out_specs=[VM] * len(shapes),
        compiler_params=pltpu.CompilerParams(vmem_limit_bytes=GRANT),
        cost_estimate=pl.CostEstimate(flops=1 << 31, bytes_accessed=moved, transcendentals=1 << 19),
    )(place, slopes, *args)


def solution(mesh):
    tokens_spec = P(("dp", "row"), "col")
    vector = P("col")
    placed = (
        tokens_spec,
        tokens_spec,
        vector,
        vector,
        P("col", "row"),
        P("row"),
        P("row", "col"),
        vector,
        vector,
        vector,
        P("col", "row"),
        P("row"),
        P("row", "col"),
        vector,
    )


    return jax.shard_map(
        local,
        mesh=mesh,
        in_specs=placed,
        out_specs=(
            tokens_spec,
            tokens_spec,
            vector,
            vector,
            P("col", "row"),
            P("row"),
            P("row", "col"),
            vector,
            vector,
            vector,
            P("col", "row"),
            P("row"),
            P("row", "col"),
            vector,
        ),
        check_vma=False,
    )
```
